256 devices in a mesh: slab: 8 (over x_lo, y), brick: 32 (over x_hi, z, core).
Axes of the slice: x: 4 (x_hi: 2, x_lo: 2; x = x_hi * 2 + x_lo), y: 4, z: 8, core: 2. Of those that a mesh axis runs over, the one named last changes fastest.
Arguments:
- embed: bfloat16 [262144, 512], P(('slab', 'brick')), may hold values from -6 to 6
- cotangent: bfloat16 [262144, 512], P(('slab', 'brick')), may hold values from -6 to 6
- basis: bfloat16 [16, 16, 262144], P(None, None, ('slab', 'brick')), may hold values from -4 to 4
- triplet_row_index: int32 [16, 262144], P(None, ('slab', 'brick')), may hold values from 0 to 1535
- triplet_slot_count: int32 [262144], P(('slab', 'brick')), may hold values from 1 to 16, as said below
- outgoing_edge_rows: int32 [4, 32768], P(None, ('slab', 'brick')), may hold values from 0 to 1023
- residual_weight: bfloat16 [512, 512], replicated, may hold values from -0.25 to 0.25
- down_weight: bfloat16 [512, 64], replicated, may hold values from -0.25 to 0.25
- up_weight: bfloat16 [64, 512], replicated, may hold values from -0.75 to 0.75
- basis_weight: bfloat16 [16, 64], replicated, may hold values from -1.5 to 1.5
Outputs:
- edge_embedding_gradient: bfloat16 [262144, 512], P(('slab', 'brick'))
- residual_weight_gradient: float32 [512, 512], replicated
- down_weight_gradient: float32 [512, 64], replicated
- up_weight_gradient: float32 [64, 512], replicated
- basis_weight_gradient: float32 [16, 64], replicated
The draws below stay inside these ranges and needn't reach their ends.
Inputs may be any that keep to these rules, and one draw needn't show every extreme that they name: `triplet_row_index`: indices refer to the extended table of the edge's own brick. `triplet_slot_count`: slots at or past the count are empty; in every brick some edge fills all 16 slots; bricks differ in density. `outgoing_edge_rows`: local row numbers within the sending brick; a row may appear more than once.
All inputs are finite; a program needn't handle non-finite values.
Results may differ from the reference program's by a relative error of at most 0.006.
Values may be sent and summed in bfloat16 or wider, within the bound.
A program may use at most 64 MiB of HBM per device.

```python
import jax
import jax.numpy as jnp
from jax import lax

D = 512
TRIPLET_WIDTH = 64
BASIS_FUNCTIONS = 16
TRIP = 16
E_DEV = 1024
GHOST = 128
EDGES = 262144
GHOSTS = 32768
N_SLAB = 8
N_BRICK = 32


def draw_triplet_slot_count(key, part):
    devices = EDGES // E_DEV
    ceiling = jax.random.randint(jax.random.fold_in(key, 11), (devices, 1), TRIP // 4, TRIP + 1)
    raw = jax.random.randint(jax.random.fold_in(key, 12), (devices, E_DEV), 0, 1048576)
    counts = 1 + raw % ceiling
    first = lax.broadcasted_iota(jnp.int32, (devices, E_DEV), 1) == 0
    return jnp.where(first, TRIP, counts).reshape(EDGES).astype(jnp.int32)


def place_ends(entries, own_key, low, largest):
    longest = entries.shape.index(max(entries.shape))
    spots = []
    for shift in (0, 1):
        where = [jax.random.randint(jax.random.fold_in(own_key, axis), (), 0, length) for axis, length in enumerate(entries.shape)]
        where[longest] = (where[longest] + shift) % entries.shape[longest]
        spots.append(tuple(where))
    return entries.at[spots[0]].set(low).at[spots[1]].set(largest)


def level_of(own_key, extent, pieces, least, top_value):
    def one(position, blocks):
        heights = jax.random.uniform(jax.random.fold_in(jax.random.fold_in(own_key, 6), position), (blocks,), jnp.float32, least / len(pieces), top_value / len(pieces))
        return jnp.repeat(jnp.exp(heights), extent[position] // blocks).reshape((-1,) + (1,) * (len(extent) - position - 1))

    gain = one(*pieces[0])
    for cut in pieces[1:]:
        gain = gain * one(*cut)
    return gain


def bell_draw(stream_key, dims, width, bound, cuts=(), kind=jnp.bfloat16):
    gain = level_of(stream_key, dims, cuts, -0.22, 0.18) if cuts else 1.0
    drawn = jax.random.normal(stream_key, dims, jnp.float32) * width * gain
    return jnp.minimum(jnp.maximum(drawn, -bound), bound).astype(kind)


def setup_inputs(seed: int = 0) -> dict:
    streams_of = jax.random.split(jax.random.key(seed), 11)
    return {
        "embed": bell_draw(streams_of[0], (EDGES, D), 1.0, 6.0, ((0, 256),)),
        "cotangent": bell_draw(streams_of[1], (EDGES, D), 1.0, 6.0, ((0, 256),)),
        "basis": bell_draw(streams_of[2], (TRIP, BASIS_FUNCTIONS, EDGES), 1.0, 4.0, ((2, 256),)),
        "triplet_row_index": place_ends(jax.random.randint(streams_of[3], (TRIP, EDGES), 0, E_DEV + 4 * GHOST), jax.random.fold_in(streams_of[3], 1), 0, (E_DEV + 4 * GHOST) - 1).astype(jnp.int32),
        "triplet_slot_count": draw_triplet_slot_count(jax.random.fold_in(streams_of[10], 71), 0),
        "outgoing_edge_rows": place_ends(jax.random.randint(streams_of[5], (4, GHOSTS), 0, E_DEV), jax.random.fold_in(streams_of[5], 1), 0, E_DEV - 1).astype(jnp.int32),
        "residual_weight": bell_draw(streams_of[6], (D, D), D ** -0.5, 0.25),
        "down_weight": bell_draw(streams_of[7], (D, TRIPLET_WIDTH), D ** -0.5, 0.25),
        "up_weight": bell_draw(streams_of[8], (TRIPLET_WIDTH, D), TRIPLET_WIDTH ** -0.5, 0.75),
        "basis_weight": bell_draw(streams_of[9], (BASIS_FUNCTIONS, TRIPLET_WIDTH), BASIS_FUNCTIONS ** -0.5, 1.5),
    }


def silu_grad(value):
    sig = jax.nn.sigmoid(value)
    return sig * (1.0 + value * (1.0 - sig))

def pick_cols(edge_table_rows, rows):
    return edge_table_rows[:, rows]

def add_cols(target, rows, values):
    return target.at[:, rows].add(values)

def reference(embed, cotangent, basis, triplet_row_index, triplet_slot_count, outgoing_edge_rows, residual_weight, down_weight, up_weight, basis_weight):
    slabs = N_SLAB
    bricks = N_BRICK
    count_dev = slabs * bricks
    pre = lax.dot_general(down_weight, embed, (((0,), (1,)), ((), ())), preferred_element_type=jnp.float32)
    proj = jax.nn.silu(pre).astype(jnp.bfloat16)
    proj_dev = proj.reshape(TRIPLET_WIDTH, slabs, bricks, E_DEV).transpose(1, 2, 0, 3)
    send = outgoing_edge_rows.reshape(4, slabs, bricks, GHOST)
    picker = jax.vmap(jax.vmap(pick_cols))
    blocks = [jnp.roll(picker(proj_dev, send[0]), 1, 0), jnp.roll(picker(proj_dev, send[1]), -1, 0), jnp.roll(picker(proj_dev, send[2]), 1, 1), jnp.roll(picker(proj_dev, send[3]), -1, 1)]
    edge_table_rows = jnp.concatenate([proj_dev] + blocks, axis=3).reshape(count_dev, TRIPLET_WIDTH, E_DEV + 4 * GHOST)
    basis_on_shard = basis.reshape(TRIP, BASIS_FUNCTIONS, count_dev, E_DEV).transpose(2, 0, 1, 3)
    slot_index_shard = triplet_row_index.reshape(TRIP, count_dev, E_DEV).transpose(1, 0, 2)
    slot_count_total = triplet_slot_count.reshape(count_dev, E_DEV)
    upstream_gradient_shard = cotangent.reshape(count_dev, E_DEV, D)
    basis_weight_float = basis_weight.astype(jnp.float32)

    def triplet_partial(inputs):
        table_d, basis_shard, index_d, count_d, cot_d = inputs
        weight_list = jnp.einsum('unz,nh->huz', basis_shard.astype(jnp.float32), basis_weight_float)
        live = (jnp.arange(TRIP)[:, None] < count_d[None, :]).astype(jnp.float32)
        gathered = table_d[:, index_d].astype(jnp.float32)
        tsum = lax.optimization_barrier(jnp.sum(weight_list * gathered * live[None], axis=1))
        activation_value = jax.nn.silu(tsum).astype(jnp.bfloat16)
        dsum = lax.dot_general(up_weight, cot_d, (((1,), (1,)), ((), ())), preferred_element_type=jnp.float32)
        dt = dsum * silu_grad(tsum)
        weight_gradient_list = (dt[:, None, :] * gathered * live[None]).astype(jnp.bfloat16)
        partial_basis_gradient = jnp.einsum('yqi,wyi->qw', basis_shard.astype(jnp.float32), weight_gradient_list.astype(jnp.float32))
        dhx = dt[:, None, :] * weight_list * live[None]
        table_gradient = jnp.zeros(table_d.shape, jnp.float32).at[:, index_d].add(dhx)
        return (table_gradient, activation_value, partial_basis_gradient)
    table_gradient, activation_value, partial_basis_gradient = lax.map(triplet_partial, (edge_table_rows, basis_on_shard, slot_index_shard, slot_count_total, upstream_gradient_shard))
    basis_weight_gradient = lax.optimization_barrier(jnp.sum(partial_basis_gradient, axis=0))
    table_gradient = table_gradient.reshape(slabs, bricks, TRIPLET_WIDTH, E_DEV + 4 * GHOST)
    dproj = table_gradient[..., :E_DEV]
    adder = jax.vmap(jax.vmap(add_cols))
    shifts = [(1, 0), (-1, 0), (1, 1), (-1, 1)]
    for step in range(4):
        by, mesh_dimension = shifts[step]
        back = table_gradient[..., E_DEV + step * GHOST:E_DEV + (step + 1) * GHOST]
        back = jnp.roll(back, -by, mesh_dimension)
        dproj = adder(dproj, send[step], back)
    dproj = dproj.transpose(2, 0, 1, 3).reshape(TRIPLET_WIDTH, EDGES)
    act_all = activation_value.transpose(1, 0, 2).reshape(TRIPLET_WIDTH, EDGES)
    up_weight_gradient = lax.dot_general(act_all, cotangent, (((1,), (0,)), ((), ())), preferred_element_type=jnp.float32)
    dpre = (dproj * silu_grad(pre)).astype(jnp.bfloat16)
    down_weight_gradient = lax.dot_general(embed, dpre, (((0,), (1,)), ((), ())), preferred_element_type=jnp.float32)
    down_term = lax.dot_general(dpre, down_weight, (((0,), (1,)), ((), ())), preferred_element_type=jnp.float32)
    res_pre = jnp.dot(embed, residual_weight, preferred_element_type=jnp.float32)
    dres = (cotangent.astype(jnp.float32) * silu_grad(res_pre)).astype(jnp.bfloat16)
    residual_weight_gradient = lax.dot_general(embed, dres, (((0,), (0,)), ((), ())), preferred_element_type=jnp.float32)
    res_term = lax.dot_general(dres, residual_weight, (((1,), (1,)), ((), ())), preferred_element_type=jnp.float32)
    edge_embedding_gradient = (res_term + down_term).astype(jnp.bfloat16)
    return (edge_embedding_gradient, residual_weight_gradient, down_weight_gradient, up_weight_gradient, basis_weight_gradient)
```

```python
import functools

import jax
import jax.numpy as jnp
from jax import lax
from jax.experimental import pallas as pl
from jax.experimental.pallas import tpu as pltpu
from jax.sharding import PartitionSpec as P

MESH = pl.DeviceIdType.MESH
DMA = pltpu.SemaphoreType.DMA


def passed_along(value, axis, steps):
    count = lax.axis_size(axis)
    pairs = [(source, (source + steps) % count) for source in range(count)]
    return lax.ppermute(value, axis, pairs)


def silu_grad(value):
    sig = jax.nn.sigmoid(value)
    return sig * (1.0 + value * (1.0 - sig))


def selector(index_row, count_rows, dtype):
    positions = lax.broadcasted_iota(jnp.int32, (count_rows, index_row.shape[0]), 0)
    return (positions == index_row[None, :]).astype(dtype)


def where_am_i():
    slab, brick = lax.axis_index("slab"), lax.axis_index("brick")
    near = lax.rem(brick, 16)
    far = slab * 2 + brick // 16
    return slab, brick, near, far


def near_peer(step):
    slab, brick, near, _ = where_am_i()
    return slab, (brick // 16) * 16 + lax.rem(near + step, 16)


def far_peer(step):
    _, _, near, far = where_am_i()
    other = lax.rem(far + step, 16)
    return other // 2, lax.rem(other, 2) * 16 + near


def z_peer(step):
    slab, brick, near, _ = where_am_i()
    return slab, (brick // 16) * 16 + lax.rem(near + 2 * step, 16)


def core_peer():
    slab, brick, _, _ = where_am_i()
    return slab, brick + 1 - 2 * lax.rem(brick, 2)


def remote(source, target, send, recv, peer):
    return pltpu.make_async_remote_copy(
        src_ref=source, dst_ref=target, send_sem=send, recv_sem=recv,
        device_id=peer, device_id_type=MESH,
    )


def each(count, body):
    def step(index, carry):
        body(index)
        return carry

    lax.fori_loop(0, count, step, 0)


class Exchange:
    def __init__(self, count, source, target, sems, peer):
        self.count, self.source, self.target, self.sems, self.peer = count, source, target, sems, peer

    def copy(self, s):
        send, recv = self.sems
        return remote(self.source(s), self.target(s), send.at[s], recv.at[s], self.peer(s + 1))

    def start(self):
        each(self.count, lambda s: self.copy(s).start())

    def arrived(self):
        each(self.count, lambda s: self.copy(s).wait_recv())

    def sent(self):
        each(self.count, lambda s: self.copy(s).wait_send())


def small_stages(own, got, mid, last, sems):
    _, _, near, far = where_am_i()
    scatter = Exchange(
        15, lambda s: own.at[lax.rem(near + s + 1, 16)], lambda s: got.at[s], sems[0], near_peer
    )
    spread = Exchange(15, lambda s: mid.at[far], lambda s: mid.at[far], sems[1], far_peer)
    gather = Exchange(15, lambda s: last.at[near], lambda s: last.at[near], sems[2], near_peer)

    def middle():
        scatter.arrived()
        total = own[near]
        for s in range(15):
            total = total + got[s]
        mid[far] = total

    def final():
        spread.arrived()
        total = mid[0]
        for s in range(1, 16):
            total = total + mid[s]
        last[near] = total.astype(last.dtype)

    return scatter, middle, spread, final, gather


def announce():
    slab, brick, _, _ = where_am_i()
    barrier = pltpu.get_barrier_semaphore()

    def tell(peer):
        pl.semaphore_signal(barrier, inc=1, device_id=peer, device_id_type=MESH)

    each(15, lambda s: tell(near_peer(s + 1)))
    each(15, lambda s: tell(far_peer(s + 1)))
    tell((slab, lax.rem(brick + 1, 32)))
    tell((slab, lax.rem(brick + 31, 32)))
    return barrier


def reduce_kernel(
    res_ref, down_ref, up_ref, basis_ref,
    res_out, down_out, up_out, basis_out,
    own, got, mid, last, basis_got, basis_mid,
    half_send, half_got, z_send, z_got, res_mid, res_last, res_other,
    sem_small, sem_basis, sem_core, sem_z, sem_far,
):
    slab, brick, near, far = where_am_i()
    core, z = lax.rem(near, 2), near // 2
    barrier = announce()
    core_rows = pl.multiple_of((1 - core) * 256, 256)
    half_send[...] = res_ref[pl.ds(core_rows, 256), :].astype(jnp.bfloat16)
    for s in range(16):
        own[s, 0:8, :] = down_ref[pl.ds(8 * (s // 2), 8), pl.ds(256 * (s % 2), 256)]
        own[s, 8:16, :] = up_ref[pl.ds(8 * (s // 2), 8), pl.ds(256 * (s % 2), 256)]
    pl.semaphore_wait(barrier, 32)
    core_first = remote(half_send, half_got, sem_core.at[0], sem_core.at[1], core_peer())
    core_first.start()
    sems = [(sem_small.at[0, t], sem_small.at[1, t]) for t in range(3)]
    scatter, middle, spread, final, gather = small_stages(own, got, mid, last, sems)
    scatter.start()
    basis_a = Exchange(15, lambda s: basis_ref, lambda s: basis_got.at[near], (sem_basis.at[0, 0], sem_basis.at[1, 0]), near_peer)
    basis_got[near] = basis_ref[...]
    basis_a.start()
    core_first.wait_recv()
    mine = pl.multiple_of(core * 256, 256)
    for t in range(8):
        rows = pl.ds(pl.multiple_of(mine + 32 * t, 32), 32)
        z_send[t] = (res_ref[rows, :] + half_got[32 * t : 32 * t + 32, :].astype(jnp.float32)).astype(jnp.bfloat16)
    z_scatter = Exchange(7, lambda s: z_send.at[lax.rem(z + s + 1, 8)], lambda s: z_got.at[s], (sem_z.at[0, 0], sem_z.at[1, 0]), z_peer)
    z_scatter.start()
    middle()
    spread.start()
    basis_a.arrived()
    basis_total = basis_got[0]
    for s in range(1, 16):
        basis_total = basis_total + basis_got[s]
    basis_mid[far] = basis_total
    basis_b = Exchange(15, lambda s: basis_mid.at[far], lambda s: basis_mid.at[far], (sem_basis.at[0, 1], sem_basis.at[1, 1]), far_peer)
    basis_b.start()
    z_scatter.arrived()
    part = res_ref[pl.ds(pl.multiple_of(mine + 32 * z, 32), 32), :] + half_got[pl.ds(pl.multiple_of(32 * z, 32), 32), :].astype(jnp.float32)
    for s in range(7):
        part = part + z_got[s].astype(jnp.float32)
    res_mid[far] = part.astype(jnp.bfloat16)
    res_spread = Exchange(15, lambda s: res_mid.at[far], lambda s: res_mid.at[far], (sem_far.at[0], sem_far.at[1]), far_peer)
    res_spread.start()
    final()
    gather.start()
    res_spread.arrived()
    part = res_mid[0].astype(jnp.float32)
    for s in range(1, 16):
        part = part + res_mid[s].astype(jnp.float32)
    res_last[pl.ds(pl.multiple_of(32 * z, 32), 32), :] = part.astype(jnp.bfloat16)
    def own_rows(s):
        return res_last.at[pl.ds(pl.multiple_of(32 * z, 32), 32), :]

    z_gather = Exchange(7, own_rows, own_rows, (sem_z.at[0, 1], sem_z.at[1, 1]), z_peer)
    z_gather.start()
    z_gather.arrived()
    core_last = remote(res_last, res_other, sem_core.at[2], sem_core.at[3], core_peer())
    core_last.start()
    res_out[pl.ds(mine, 256), :] = res_last[...].astype(jnp.float32)
    gather.arrived()
    for s in range(16):
        down_out[8 * (s // 2) : 8 * (s // 2) + 8, 256 * (s % 2) : 256 * (s % 2) + 256] = last[s, 0:8, :].astype(jnp.float32)
        up_out[8 * (s // 2) : 8 * (s // 2) + 8, 256 * (s % 2) : 256 * (s % 2) + 256] = last[s, 8:16, :].astype(jnp.float32)
    basis_b.arrived()
    basis_total = basis_mid[0]
    for s in range(1, 16):
        basis_total = basis_total + basis_mid[s]
    basis_out[...] = basis_total
    core_last.wait_recv()
    res_out[pl.ds(core_rows, 256), :] = res_other[...].astype(jnp.float32)
    for exchange in (scatter, spread, gather, basis_a, basis_b, z_scatter, res_spread, z_gather):
        exchange.sent()
    core_first.wait_send()
    core_last.wait_send()


def reduce_all(res, down, up, basis):
    f32, bf16 = jnp.float32, jnp.bfloat16
    return pl.pallas_call(
        reduce_kernel,
        out_shape=(
            jax.ShapeDtypeStruct((512, 512), f32),
            jax.ShapeDtypeStruct((64, 512), f32),
            jax.ShapeDtypeStruct((64, 512), f32),
            jax.ShapeDtypeStruct((16, 64), f32),
        ),
        in_specs=[pl.BlockSpec(memory_space=pltpu.VMEM)] * 4,
        out_specs=[pl.BlockSpec(memory_space=pltpu.VMEM)] * 4,
        scratch_shapes=[
            pltpu.VMEM((16, 16, 256), f32),
            pltpu.VMEM((15, 16, 256), f32),
            pltpu.VMEM((16, 16, 256), f32),
            pltpu.VMEM((16, 16, 256), bf16),
            pltpu.VMEM((16, 16, 64), f32),
            pltpu.VMEM((16, 16, 64), f32),
            pltpu.VMEM((256, 512), bf16),
            pltpu.VMEM((256, 512), bf16),
            pltpu.VMEM((8, 32, 512), bf16),
            pltpu.VMEM((7, 32, 512), bf16),
            pltpu.VMEM((16, 32, 512), bf16),
            pltpu.VMEM((256, 512), bf16),
            pltpu.VMEM((256, 512), bf16),
            DMA((2, 3, 15)),
            DMA((2, 2, 15)),
            DMA((4,)),
            DMA((2, 2, 7)),
            DMA((2, 15)),
        ],
        compiler_params=pltpu.CompilerParams(collective_id=0, has_side_effects=True),
        name="reduce_all",
    )(res, down, up, basis)


def shards(
    embed,
    cotangent,
    basis,
    triplet_row_index,
    triplet_slot_count,
    outgoing_edge_rows,
    residual_weight,
    down_weight,
    up_weight,
    basis_weight,
):
    rows = embed.shape[0]
    ghost = outgoing_edge_rows.shape[1]
    trips = triplet_row_index.shape[0]
    res_pre = jnp.dot(embed, residual_weight, preferred_element_type=jnp.float32)
    dres = (cotangent.astype(jnp.float32) * silu_grad(res_pre)).astype(jnp.bfloat16)
    residual_weight_gradient = lax.dot_general(
        embed, dres, (((0,), (0,)), ((), ())), preferred_element_type=jnp.float32
    )
    res_term = lax.dot_general(
        dres, residual_weight, (((1,), (1,)), ((), ())), preferred_element_type=jnp.float32
    )
    pre = lax.dot_general(
        down_weight, embed, (((0,), (1,)), ((), ())), preferred_element_type=jnp.float32
    )
    proj = jax.nn.silu(pre).astype(jnp.bfloat16)
    picks = [selector(outgoing_edge_rows[step], rows, jnp.bfloat16) for step in range(4)]
    received = []
    for step, by in enumerate((1, -1)):
        chosen = jnp.dot(proj, picks[step], preferred_element_type=jnp.float32).astype(jnp.bfloat16)
        received.append(passed_along(chosen, "slab", by))
    for step, by in enumerate((1, -1)):
        chosen = jnp.dot(proj, picks[step + 2], preferred_element_type=jnp.float32).astype(
            jnp.bfloat16
        )
        received.append(passed_along(chosen, "brick", by))
    ghost_proj = jnp.concatenate(received, axis=1)
    edge_table_rows = jnp.concatenate([proj, ghost_proj], axis=1)
    table_rows = edge_table_rows.shape[1]
    weight_list = jnp.einsum("unz,nh->uhz", basis, basis_weight, preferred_element_type=jnp.float32)
    live = (lax.broadcasted_iota(jnp.int32, (trips, rows), 0) < triplet_slot_count[None, :]).astype(
        jnp.float32
    )

    def gather_slot(carry, index_row):
        onehot = selector(index_row, table_rows, jnp.bfloat16)
        picked = jnp.dot(edge_table_rows, onehot, preferred_element_type=jnp.float32).astype(
            jnp.bfloat16
        )
        return (carry, picked)

    _, gathered = lax.scan(gather_slot, jnp.zeros((), jnp.float32), triplet_row_index)
    gathered = gathered.astype(jnp.float32)
    tsum = jnp.sum(weight_list * gathered * live[:, None, :], axis=0)
    activation_value = jax.nn.silu(tsum).astype(jnp.bfloat16)
    dsum = lax.dot_general(
        up_weight, cotangent, (((1,), (1,)), ((), ())), preferred_element_type=jnp.float32
    )
    dt = dsum * silu_grad(tsum)
    up_weight_gradient = lax.dot_general(
        activation_value, cotangent, (((1,), (0,)), ((), ())), preferred_element_type=jnp.float32
    )
    weight_gradient_list = (dt[None, :, :] * gathered * live[:, None, :]).astype(jnp.bfloat16)
    basis_weight_gradient = jnp.einsum(
        "yqi,ywi->qw", basis, weight_gradient_list, preferred_element_type=jnp.float32
    )
    dhx = dt[None, :, :] * weight_list * live[:, None, :]

    def scatter_slot(total, inputs):
        index_row, slot_terms = inputs
        onehot = selector(index_row, table_rows, jnp.bfloat16)
        added = lax.dot_general(
            slot_terms.astype(jnp.bfloat16),
            onehot,
            (((1,), (1,)), ((), ())),
            preferred_element_type=jnp.float32,
        )
        return (total + added, None)

    table_gradient, _ = lax.scan(
        scatter_slot,
        jnp.zeros((edge_table_rows.shape[0], table_rows), jnp.float32),
        (triplet_row_index, dhx),
    )
    dproj = table_gradient[:, :rows]
    for step, by in enumerate((1, -1)):
        block = table_gradient[:, rows + step * ghost : rows + (step + 1) * ghost]
        back = passed_along(block, "slab", -by)
        dproj = dproj + lax.dot_general(
            back,
            picks[step].astype(jnp.float32),
            (((1,), (1,)), ((), ())),
            precision=lax.Precision.HIGHEST,
            preferred_element_type=jnp.float32,
        )
    for step, by in enumerate((1, -1)):
        block = table_gradient[:, rows + (step + 2) * ghost : rows + (step + 3) * ghost]
        back = passed_along(block, "brick", -by)
        dproj = dproj + lax.dot_general(
            back,
            picks[step + 2].astype(jnp.float32),
            (((1,), (1,)), ((), ())),
            precision=lax.Precision.HIGHEST,
            preferred_element_type=jnp.float32,
        )
    dpre = (dproj * silu_grad(pre)).astype(jnp.bfloat16)
    down_weight_gradient = lax.dot_general(
        dpre, embed, (((1,), (0,)), ((), ())), preferred_element_type=jnp.float32
    )
    down_term = lax.dot_general(
        dpre, down_weight, (((0,), (1,)), ((), ())), preferred_element_type=jnp.float32
    )
    edge_embedding_gradient = (res_term + down_term).astype(jnp.bfloat16)
    reduced_total = reduce_all(
        residual_weight_gradient, down_weight_gradient, up_weight_gradient, basis_weight_gradient
    )
    return (
        edge_embedding_gradient,
        reduced_total[0],
        reduced_total[1].T,
        reduced_total[2],
        reduced_total[3],
    )


def solution(mesh):
    in_specs = (
        P(("slab", "brick"), None),
        P(("slab", "brick"), None),
        P(None, None, ("slab", "brick")),
        P(None, ("slab", "brick")),
        P(("slab", "brick")),
        P(None, ("slab", "brick")),
        P(),
        P(),
        P(),
        P(),
    )
    out_specs = (P(("slab", "brick"), None), P(), P(), P(), P())
    return jax.shard_map(shards, mesh=mesh, in_specs=in_specs, out_specs=out_specs, check_vma=False)
```

```python
import functools

import jax
import jax.numpy as jnp
from jax import lax
from jax.experimental import pallas as pl
from jax.experimental.pallas import tpu as pltpu
from jax.sharding import PartitionSpec as P

MESH = pl.DeviceIdType.MESH
DMA = pltpu.SemaphoreType.DMA


def where_am_i():
    slab, brick = lax.axis_index("slab"), lax.axis_index("brick")
    near = lax.rem(brick, 16)
    far = slab * 2 + brick // 16
    return slab, brick, near, far


def near_peer(step):
    slab, brick, near, _ = where_am_i()
    return slab, (brick // 16) * 16 + lax.rem(near + step, 16)


def far_peer(step):
    _, _, near, far = where_am_i()
    other = lax.rem(far + step, 16)
    return other // 2, lax.rem(other, 2) * 16 + near


def z_peer(step):
    slab, brick, near, _ = where_am_i()
    return slab, (brick // 16) * 16 + lax.rem(near + 2 * step, 16)


def core_peer():
    slab, brick, _, _ = where_am_i()
    return slab, brick + 1 - 2 * lax.rem(brick, 2)


def remote(source, target, send, recv, peer):
    return pltpu.make_async_remote_copy(
        src_ref=source, dst_ref=target, send_sem=send, recv_sem=recv,
        device_id=peer, device_id_type=MESH,
    )


def each(count, body):
    def step(index, carry):
        body(index)
        return carry

    lax.fori_loop(0, count, step, 0)


class Exchange:
    def __init__(self, count, source, target, sems, peer):
        self.count, self.source, self.target, self.sems, self.peer = count, source, target, sems, peer

    def copy(self, s):
        send, recv = self.sems
        return remote(self.source(s), self.target(s), send.at[s], recv.at[s], self.peer(s + 1))

    def start(self):
        each(self.count, lambda s: self.copy(s).start())

    def arrived(self):
        each(self.count, lambda s: self.copy(s).wait_recv())

    def sent(self):
        each(self.count, lambda s: self.copy(s).wait_send())


def small_stages(own, got, mid, last, sems):
    _, _, near, far = where_am_i()
    scatter = Exchange(
        15, lambda s: own.at[lax.rem(near + s + 1, 16)], lambda s: got.at[s], sems[0], near_peer
    )
    spread = Exchange(15, lambda s: mid.at[far], lambda s: mid.at[far], sems[1], far_peer)
    gather = Exchange(15, lambda s: last.at[near], lambda s: last.at[near], sems[2], near_peer)

    def middle():
        scatter.arrived()
        total = own[near]
        for s in range(15):
            total = total + got[s]
        mid[far] = total

    def final():
        spread.arrived()
        total = mid[0]
        for s in range(1, 16):
            total = total + mid[s]
        last[near] = total.astype(last.dtype)

    return scatter, middle, spread, final, gather


def announce():
    slab, brick, _, _ = where_am_i()
    barrier = pltpu.get_barrier_semaphore()

    def tell(peer):
        pl.semaphore_signal(barrier, inc=1, device_id=peer, device_id_type=MESH)

    each(15, lambda s: tell(near_peer(s + 1)))
    each(15, lambda s: tell(far_peer(s + 1)))
    tell((slab, lax.rem(brick + 1, 32)))
    tell((slab, lax.rem(brick + 31, 32)))
    return barrier


F32, BF16 = jnp.float32, jnp.bfloat16


def sigmoid(value):
    return 0.5 * jnp.tanh(0.5 * value) + 0.5


def silu_grad(value):
    sig = sigmoid(value)
    return sig * (1.0 + value * (1.0 - sig))


def dot(a, b, ca=1, cb=0):
    return lax.dot_general(a, b, (((ca,), (cb,)), ((), ())), preferred_element_type=F32)


def low_onehot(low):
    width = low.shape[1]
    positions = lax.broadcasted_iota(jnp.int32, (256, width), 0)
    return jnp.where(positions == low, 1.0, 0.0).astype(BF16)


def slice_of(s):
    return pl.ds(8 * (s // 2), 8), pl.ds(256 * (s % 2), 256)


def fused_kernel(
    embed, cot, basis, index, count, rows_out, w_res, w_down, w_up, w_basis,
    edge_out, res_out, down_out, up_out, basis_out,
    table, pre, ghost_send, ghost_hot, down_t, dres, res_sum, wts, dsum,
    hot, picked, tsum, dt, table_sum, back_send, back_got, dpre,
    own_d, got_d, mid_d, last_d, own_u, got_u, mid_u, last_u, basis_got, basis_mid,
    half_send, half_got, z_send, z_got, res_mid, res_last, res_other,
    sem_ghost, sem_back, sem_d, sem_u, sem_basis, sem_core, sem_z, sem_far,
):
    slab, brick, near, far = where_am_i()
    core, z = lax.rem(near, 2), near // 2
    ahead = ((lax.rem(slab + 1, 8), brick), (lax.rem(slab + 7, 8), brick),
             (slab, lax.rem(brick + 1, 32)), (slab, lax.rem(brick + 31, 32)))
    behind = (ahead[1], ahead[0], ahead[3], ahead[2])
    barrier = announce()

    down_t[...] = w_down[...].astype(F32).T.astype(BF16)
    pre_all = dot(down_t[...], embed[...], 1, 1)
    for c in range(4):
        part = pre_all[:, 256 * c : 256 * c + 256]
        pre[64 * c : 64 * c + 64, :] = part
        table[64 * c : 64 * c + 64, :] = (part * sigmoid(part)).astype(BF16)
    for k in range(4):
        sent = rows_out[k : k + 1, :]
        lanes = pl.ds(128 * k, 128)
        ghost_hot[:, lanes] = low_onehot(jnp.bitwise_and(sent, 255))
        wide = dot(table[0:256, :], ghost_hot[:, lanes])
        chunk = jnp.right_shift(sent, 8)
        chosen = wide[0:64]
        for c in range(1, 4):
            chosen = jnp.where(chunk == c, wide[64 * c : 64 * c + 64], chosen)
        ghost_send[k] = chosen.astype(BF16)
    pl.semaphore_wait(barrier, 32)

    def ghost_copy(k):
        place = table.at[pl.ds(256 + 64 * (k // 2), 64), pl.ds(128 * (k % 2), 128)]
        return remote(ghost_send.at[k], place, sem_ghost.at[0, k], sem_ghost.at[1, k], ahead[k])

    for k in range(4):
        ghost_copy(k).start()

    def residual(i):
        rows = pl.ds(pl.multiple_of(256 * i, 256), 256)
        value = dot(embed[rows, :], w_res[...])
        dres[rows, :] = (cot[rows, :].astype(F32) * silu_grad(value)).astype(BF16)

    each(4, residual)

    def residual_grad(i):
        rows = pl.ds(pl.multiple_of(128 * i, 128), 128)
        res_sum[rows, :] = dot(embed[:, rows], dres[...], 0, 0)

    each(4, residual_grad)
    other_half = pl.ds(pl.multiple_of((1 - core) * 256, 256), 256)
    half_send[...] = res_sum[other_half, :].astype(BF16)
    core_first = remote(half_send, half_got, sem_core.at[0], sem_core.at[1], core_peer())
    core_first.start()

    spread_n = (lax.broadcasted_iota(jnp.int32, (16, 256), 1) % 16) == lax.broadcasted_iota(jnp.int32, (16, 256), 0)
    wide_w = dot(w_basis[...], jnp.where(spread_n, 1.0, 0.0).astype(BF16), 0, 0)
    lane_slot = lax.broadcasted_iota(jnp.int32, (64, 256), 1) // 16
    for j in range(16):
        wts[j] = dot(jnp.where(lane_slot == j, wide_w, 0.0).astype(BF16), basis[...])
    dsum[...] = dot(w_up[...], cot[...], 1, 1)

    core_first.wait_recv()
    mine = pl.multiple_of(core * 256, 256)

    def to_z(t):
        rows = pl.ds(pl.multiple_of(mine + 32 * t, 32), 32)
        got = half_got[pl.ds(pl.multiple_of(32 * t, 32), 32), :]
        z_send[t] = (res_sum[rows, :] + got.astype(F32)).astype(BF16)

    each(8, to_z)
    z_scatter = Exchange(
        7, lambda s: z_send.at[lax.rem(z + s + 1, 8)], lambda s: z_got.at[s], (sem_z.at[0, 0], sem_z.at[1, 0]), z_peer
    )
    z_scatter.start()
    for k in range(4):
        ghost_copy(k).wait_recv()

    tsum[...] = jnp.zeros_like(tsum)

    def gather(j):
        row = index[pl.ds(j, 1), :]
        low = jnp.where(j < count[...], jnp.bitwise_and(row, 255), -1)
        chunk = jnp.right_shift(row, 8)
        hot[j] = low_onehot(low)
        wide = dot(table[...], hot[j])
        chosen = wide[0:64]
        for c in range(1, 6):
            chosen = jnp.where(chunk == c, wide[64 * c : 64 * c + 64], chosen)
        picked[j] = chosen.astype(BF16)
        tsum[...] += wts[j] * chosen

    each(16, gather)

    z_scatter.arrived()
    mine_z = pl.ds(pl.multiple_of(32 * z, 32), 32)
    part = res_sum[pl.ds(pl.multiple_of(mine + 32 * z, 32), 32), :] + half_got[mine_z, :].astype(F32)
    for s in range(7):
        part = part + z_got[s].astype(F32)
    res_mid[far] = part.astype(BF16)
    res_spread = Exchange(15, lambda s: res_mid.at[far], lambda s: res_mid.at[far], (sem_far.at[0], sem_far.at[1]), far_peer)
    res_spread.start()

    total = tsum[...]
    act = (total * sigmoid(total)).astype(BF16)
    dt[...] = dsum[...] * silu_grad(total)
    up_grad = dot(act, cot[...])
    for s in range(16):
        own_u[s] = up_grad[8 * (s // 2) : 8 * (s // 2) + 8, 256 * (s % 2) : 256 * (s % 2) + 256]
    sems_u = [(sem_u.at[0, t], sem_u.at[1, t]) for t in range(3)]
    scatter_u, middle_u, spread_u, final_u, gather_u = small_stages(own_u, got_u, mid_u, last_u, sems_u)
    scatter_u.start()

    table_sum[...] = jnp.zeros_like(table_sum)

    def scatter(j):
        chunk = jnp.right_shift(index[pl.ds(j, 1), :], 8)
        slope = dt[...]
        term = (slope * wts[j]).astype(BF16)
        picked[j] = (slope * picked[j].astype(F32)).astype(BF16)
        parts = [term * jnp.where(chunk == c, 1.0, 0.0).astype(BF16) for c in range(6)]
        table_sum[...] += dot(jnp.concatenate(parts, axis=0), hot[j], 1, 1)

    each(16, scatter)

    def back_copy(k):
        return remote(back_send.at[k], back_got.at[k], sem_back.at[0, k], sem_back.at[1, k], behind[k])

    for k in range(4):
        back_send[k] = table_sum[256 + 64 * (k // 2) : 320 + 64 * (k // 2), 128 * (k % 2) : 128 * (k % 2) + 128].astype(BF16)
        back_copy(k).start()

    basis_grad = jnp.zeros((16, 64), F32)
    for j in range(16):
        basis_grad = basis_grad + dot(basis[16 * j : 16 * j + 16, :], picked[j], 1, 1)
    basis_got[near] = basis_grad
    basis_a = Exchange(15, lambda s: basis_got.at[near], lambda s: basis_got.at[near], (sem_basis.at[0, 0], sem_basis.at[1, 0]), near_peer)
    basis_a.start()

    middle_u()
    spread_u.start()
    res_spread.arrived()
    part = res_mid[0].astype(F32)
    for s in range(1, 16):
        part = part + res_mid[s].astype(F32)
    res_last[mine_z, :] = part.astype(BF16)
    z_gather = Exchange(7, lambda s: res_last.at[mine_z, :], lambda s: res_last.at[mine_z, :], (sem_z.at[0, 1], sem_z.at[1, 1]), z_peer)
    z_gather.start()

    for k in range(4):
        back_copy(k).wait_recv()
    returned = table_sum[0:256, :]
    for k in range(4):
        chunk = jnp.right_shift(rows_out[k : k + 1, :], 8)
        term = back_got[k]
        parts = [term * jnp.where(chunk == c, 1.0, 0.0).astype(BF16) for c in range(4)]
        returned = returned + dot(jnp.concatenate(parts, axis=0), ghost_hot[:, 128 * k : 128 * k + 128], 1, 1)
    returned = (returned * silu_grad(pre[...])).astype(BF16)
    for c in range(4):
        dpre[:, 256 * c : 256 * c + 256] = returned[64 * c : 64 * c + 64, :]
    down_grad = dot(dpre[...], embed[...])
    for s in range(16):
        own_d[s] = down_grad[8 * (s // 2) : 8 * (s // 2) + 8, 256 * (s % 2) : 256 * (s % 2) + 256]
    sems_d = [(sem_d.at[0, t], sem_d.at[1, t]) for t in range(3)]
    scatter_d, middle_d, spread_d, final_d, gather_d = small_stages(own_d, got_d, mid_d, last_d, sems_d)
    scatter_d.start()

    basis_a.arrived()
    basis_total = basis_got[0]
    for s in range(1, 16):
        basis_total = basis_total + basis_got[s]
    basis_mid[far] = basis_total
    basis_b = Exchange(15, lambda s: basis_mid.at[far], lambda s: basis_mid.at[far], (sem_basis.at[0, 1], sem_basis.at[1, 1]), far_peer)
    basis_b.start()

    def edge(i):
        rows = pl.ds(pl.multiple_of(256 * i, 256), 256)
        value = dot(dres[rows, :], w_res[...], 1, 1) + dot(dpre[:, rows], down_t[...], 0, 0)
        edge_out[rows, :] = value.astype(BF16)

    each(4, edge)

    middle_d()
    spread_d.start()
    final_u()
    gather_u.start()
    z_gather.arrived()
    core_last = remote(res_last, res_other, sem_core.at[2], sem_core.at[3], core_peer())
    core_last.start()
    res_out[pl.ds(mine, 256), :] = res_last[...].astype(F32)
    final_d()
    gather_d.start()
    basis_b.arrived()
    basis_total = basis_mid[0]
    for s in range(1, 16):
        basis_total = basis_total + basis_mid[s]
    basis_out[...] = basis_total
    gather_u.arrived()
    for s in range(16):
        up_out[8 * (s // 2) : 8 * (s // 2) + 8, 256 * (s % 2) : 256 * (s % 2) + 256] = last_u[s].astype(F32)
    core_last.wait_recv()
    res_out[other_half, :] = res_other[...].astype(F32)
    for k in range(4):
        ghost_copy(k).wait_send()
        back_copy(k).wait_send()
    for exchange in (scatter_u, spread_u, gather_u, scatter_d, spread_d, basis_a, basis_b, z_scatter, res_spread, z_gather):
        exchange.sent()
    core_first.wait_send()
    core_last.wait_send()
    gather_d.arrived()
    for r in range(8):
        block = jnp.concatenate([last_d[2 * r], last_d[2 * r + 1]], axis=1)
        dpre[8 * r : 8 * r + 8, 0:512] = block
    down_out[...] = dpre[:, 0:512].astype(F32).T
    gather_d.sent()


def shards(
    embed, cotangent, basis, triplet_row_index, triplet_slot_count, outgoing_edge_rows,
    residual_weight, down_weight, up_weight, basis_weight,
):
    vmem = pltpu.VMEM
    return pl.pallas_call(
        fused_kernel,
        out_shape=(
            jax.ShapeDtypeStruct((1024, 512), BF16),
            jax.ShapeDtypeStruct((512, 512), F32),
            jax.ShapeDtypeStruct((512, 64), F32),
            jax.ShapeDtypeStruct((64, 512), F32),
            jax.ShapeDtypeStruct((16, 64), F32),
        ),
        in_specs=[pl.BlockSpec(memory_space=vmem)] * 10,
        out_specs=[pl.BlockSpec(memory_space=vmem)] * 5,
        scratch_shapes=[
            vmem((384, 256), BF16),
            vmem((256, 256), F32),
            vmem((4, 64, 128), BF16),
            vmem((256, 512), BF16),
            vmem((64, 512), BF16),
            vmem((1024, 512), BF16),
            vmem((512, 512), F32),
            vmem((16, 64, 1024), F32),
            vmem((64, 1024), F32),
            vmem((16, 256, 1024), BF16),
            vmem((16, 64, 1024), BF16),
            vmem((64, 1024), F32),
            vmem((64, 1024), F32),
            vmem((384, 256), F32),
            vmem((4, 64, 128), BF16),
            vmem((4, 64, 128), BF16),
            vmem((64, 1024), BF16),
            vmem((16, 8, 256), F32),
            vmem((15, 8, 256), F32),
            vmem((16, 8, 256), F32),
            vmem((16, 8, 256), BF16),
            vmem((16, 8, 256), F32),
            vmem((15, 8, 256), F32),
            vmem((16, 8, 256), F32),
            vmem((16, 8, 256), BF16),
            vmem((16, 16, 64), F32),
            vmem((16, 16, 64), F32),
            vmem((256, 512), BF16),
            vmem((256, 512), BF16),
            vmem((8, 32, 512), BF16),
            vmem((7, 32, 512), BF16),
            vmem((16, 32, 512), BF16),
            vmem((256, 512), BF16),
            vmem((256, 512), BF16),
            DMA((2, 4)),
            DMA((2, 4)),
            DMA((2, 3, 15)),
            DMA((2, 3, 15)),
            DMA((2, 2, 15)),
            DMA((4,)),
            DMA((2, 2, 7)),
            DMA((2, 15)),
        ],
        compiler_params=pltpu.CompilerParams(
            collective_id=0, has_side_effects=True, vmem_limit_bytes=60 * 1024 * 1024
        ),
        name="fused",
    )(
        embed, cotangent, basis.reshape(256, 1024), triplet_row_index, triplet_slot_count.reshape(1, 1024),
        outgoing_edge_rows, residual_weight, down_weight, up_weight, basis_weight,
    )


def solution(mesh):
    in_specs = (
        P(("slab", "brick"), None),
        P(("slab", "brick"), None),
        P(None, None, ("slab", "brick")),
        P(None, ("slab", "brick")),
        P(("slab", "brick")),
        P(None, ("slab", "brick")),
        P(),
        P(),
        P(),
        P(),
    )
    out_specs = (P(("slab", "brick"), None), P(), P(), P(), P())
    return jax.shard_map(shards, mesh=mesh, in_specs=in_specs, out_specs=out_specs, check_vma=False)
```

```python
import functools

import jax
import jax.numpy as jnp
from jax import lax
from jax.experimental import pallas as pl
from jax.experimental.pallas import tpu as pltpu
from jax.sharding import PartitionSpec as P

MESH = pl.DeviceIdType.MESH
DMA = pltpu.SemaphoreType.DMA


def where_am_i():
    slab, brick = lax.axis_index("slab"), lax.axis_index("brick")
    near = lax.rem(brick, 16)
    far = slab * 2 + brick // 16
    return slab, brick, near, far


def near_peer(step):
    slab, brick, near, _ = where_am_i()
    return slab, (brick // 16) * 16 + lax.rem(near + step, 16)


def far_peer(step):
    _, _, near, far = where_am_i()
    other = lax.rem(far + step, 16)
    return other // 2, lax.rem(other, 2) * 16 + near


def z_peer(step):
    slab, brick, near, _ = where_am_i()
    return slab, (brick // 16) * 16 + lax.rem(near + 2 * step, 16)


def core_peer():
    slab, brick, _, _ = where_am_i()
    return slab, brick + 1 - 2 * lax.rem(brick, 2)


def remote(source, target, send, recv, peer):
    return pltpu.make_async_remote_copy(
        src_ref=source, dst_ref=target, send_sem=send, recv_sem=recv,
        device_id=peer, device_id_type=MESH,
    )


def each(count, body, unroll=1):
    def step(index, carry):
        body(index)
        return carry

    lax.fori_loop(0, count, step, 0, unroll=unroll)


class Exchange:
    def __init__(self, count, source, target, gone, came, sems, peer):
        self.count, self.source, self.target, self.gone, self.came = count, source, target, gone, came
        self.sems, self.peer = sems, peer

    def start(self):
        send, recv = self.sems
        each(self.count, lambda s: remote(self.source(s), self.target(s), send, recv, self.peer(s + 1)).start())

    def arrived(self):
        pltpu.make_async_copy(self.came, self.came, self.sems[1]).wait()

    def sent(self):
        pltpu.make_async_copy(self.gone, self.gone, self.sems[0]).wait()


def small_stages(own, got, mid, last, sems):
    _, _, near, far = where_am_i()
    scatter = Exchange(
        15, lambda s: own.at[lax.rem(far + s + 1, 16)], lambda s: got.at[s], got, got, sems[0], far_peer
    )
    spread = Exchange(15, lambda s: mid.at[near], lambda s: mid.at[near], mid.at[0:15], mid.at[0:15], sems[1], near_peer)
    gather = Exchange(15, lambda s: last.at[far], lambda s: last.at[far], last.at[0:15], last.at[0:15], sems[2], far_peer)

    def middle():
        scatter.arrived()
        total = own[far]
        for s in range(15):
            total = total + got[s]
        mid[near] = total

    def final():
        spread.arrived()
        total = mid[0]
        for s in range(1, 16):
            total = total + mid[s]
        last[far] = total.astype(last.dtype)

    return scatter, middle, spread, final, gather


def announce():
    slab, brick, _, _ = where_am_i()
    barrier = pltpu.get_barrier_semaphore()

    def tell(peer):
        pl.semaphore_signal(barrier, inc=1, device_id=peer, device_id_type=MESH)

    each(15, lambda s: tell(near_peer(s + 1)))
    each(15, lambda s: tell(far_peer(s + 1)))
    tell((slab, lax.rem(brick + 1, 32)))
    tell((slab, lax.rem(brick + 31, 32)))
    return barrier


F32, BF16 = jnp.float32, jnp.bfloat16


def sigmoid(value):
    return 0.5 * jnp.tanh(0.5 * value) + 0.5


def silu_grad(value):
    sig = sigmoid(value)
    return sig * (1.0 + value * (1.0 - sig))


def dot(a, b, ca=1, cb=0):
    return lax.dot_general(a, b, (((ca,), (cb,)), ((), ())), preferred_element_type=F32)


def low_onehot(low):
    width = low.shape[1]
    positions = lax.broadcasted_iota(jnp.int32, (256, width), 0)
    return jnp.where(positions == low, 1.0, 0.0).astype(BF16)


def slice_of(s):
    return pl.ds(8 * (s // 2), 8), pl.ds(256 * (s % 2), 256)


def fused_kernel(
    embed_hbm, cot_hbm, basis_hbm, index_hbm, count_hbm, rows_hbm, w_res_hbm, down_hbm, w_up_hbm, w_basis_hbm,
    edge_hbm, res_hbm, small_out,
    embed, cot, basis, index, count, rows_out, w_res, down_t, w_up, w_basis,
    table, pre, ghost_send, ghost_hot, dres, res_sum, wts, dsum,
    hot, picked, tsum, dt, table_sum, back_send, back_got, dpre,
    own_d, got_d, mid_d, last_d, own_u, got_u, mid_u, last_u, basis_got, basis_mid,
    half_send, half_got, far_send, far_got, res_mid, res_last, res_other,
    sem_ghost, sem_back, sem_d, sem_u, sem_basis, sem_core, sem_z, sem_far, sem_in, sem_out, edge_out, res_out,
):
    slab, brick, near, far = where_am_i()
    core, z = lax.rem(near, 2), near // 2
    ahead = ((lax.rem(slab + 1, 8), brick), (lax.rem(slab + 7, 8), brick),
             (slab, lax.rem(brick + 1, 32)), (slab, lax.rem(brick + 31, 32)))
    behind = (ahead[1], ahead[0], ahead[3], ahead[2])
    loads = {}
    for place, (name, source, target) in enumerate((
        ("embed", embed_hbm, embed), ("down", down_hbm, down_t), ("rows", rows_hbm, rows_out), ("w_res", w_res_hbm, w_res),
        ("cot", cot_hbm, cot), ("basis", basis_hbm, basis), ("w_basis", w_basis_hbm, w_basis), ("w_up", w_up_hbm, w_up),
        ("index", index_hbm, index), ("count", count_hbm, count),
    )):
        loads[name] = pltpu.make_async_copy(source, target, sem_in.at[place])
    for name in ("embed", "down", "rows"):
        loads[name].start()
    barrier = announce()
    for name in ("w_res", "cot", "basis", "w_basis", "w_up", "index", "count"):
        loads[name].start()

    loads["down"].wait()
    loads["embed"].wait()
    pre_all = dot(down_t[...], embed[...], 1, 1)
    for c in range(4):
        part = pre_all[:, 256 * c : 256 * c + 256]
        pre[64 * c : 64 * c + 64, :] = part
        table[64 * c : 64 * c + 64, :] = (part * sigmoid(part)).astype(BF16)
    loads["rows"].wait()
    for k in range(4):
        sent = rows_out[k : k + 1, :]
        lanes = pl.ds(128 * k, 128)
        ghost_hot[:, lanes] = low_onehot(jnp.bitwise_and(sent, 255))
        wide = dot(table[0:256, :], ghost_hot[:, lanes])
        chunk = jnp.right_shift(sent, 8)
        chosen = wide[0:64]
        for c in range(1, 4):
            chosen = jnp.where(chunk == c, wide[64 * c : 64 * c + 64], chosen)
        ghost_send[k] = chosen.astype(BF16)
    loads["w_res"].wait()
    loads["cot"].wait()

    def residual(i):
        rows = pl.ds(pl.multiple_of(256 * i, 256), 256)
        value = dot(embed[rows, :], w_res[...])
        dres[rows, :] = (cot[rows, :].astype(F32) * silu_grad(value)).astype(BF16)

    each(4, residual)

    def residual_grad(i):
        rows = pl.ds(pl.multiple_of(128 * i, 128), 128)
        res_sum[rows, :] = dot(embed[:, rows], dres[...], 0, 0)

    each(4, residual_grad)
    other_half = pl.ds(pl.multiple_of((1 - core) * 256, 256), 256)
    half_send[...] = res_sum[other_half, :].astype(BF16)
    pl.semaphore_wait(barrier, 32)

    def ghost_copy(k):
        place = table.at[pl.ds(256 + 64 * (k // 2), 64), pl.ds(128 * (k % 2), 128)]
        return remote(ghost_send.at[k], place, sem_ghost.at[0], sem_ghost.at[1], ahead[k])

    for k in range(4):
        ghost_copy(k).start()

    core_first = remote(half_send, half_got, sem_core.at[0], sem_core.at[1], core_peer())
    core_first.start()

    for name in ("basis", "w_basis", "w_up", "index", "count"):
        loads[name].wait()
    spread_n = (lax.broadcasted_iota(jnp.int32, (16, 256), 1) % 16) == lax.broadcasted_iota(jnp.int32, (16, 256), 0)
    wide_w = dot(w_basis[...], jnp.where(spread_n, 1.0, 0.0).astype(BF16), 0, 0)
    lane_slot = lax.broadcasted_iota(jnp.int32, (64, 256), 1) // 16
    for j in range(16):
        wts[j] = dot(jnp.where(lane_slot == j, wide_w, 0.0).astype(BF16), basis[...])
    dsum[...] = dot(w_up[...], cot[...], 1, 1)

    core_first.wait_recv()
    mine = pl.multiple_of(core * 256, 256)

    def to_far(t):
        rows = pl.ds(pl.multiple_of(mine + 16 * t, 16), 16)
        got = half_got[pl.ds(pl.multiple_of(16 * t, 16), 16), :]
        far_send[t] = (res_sum[rows, :] + got.astype(F32)).astype(BF16)

    each(16, to_far)
    res_scatter = Exchange(
        15, lambda s: far_send.at[lax.rem(far + s + 1, 16)], lambda s: far_got.at[s], far_got, far_got, (sem_far.at[0, 0], sem_far.at[1, 0]), far_peer
    )
    res_scatter.start()
    pltpu.make_async_copy(ghost_send, ghost_send, sem_ghost.at[1]).wait()

    tsum[...] = jnp.zeros_like(tsum)

    def gather(j):
        row = index[pl.ds(j, 1), :]
        low = jnp.where(j < count[...], jnp.bitwise_and(row, 255), -1)
        chunk = jnp.right_shift(row, 8)
        hot[j] = low_onehot(low)
        wide = dot(table[...], hot[j])
        chosen = wide[0:64]
        for c in range(1, 6):
            chosen = jnp.where(chunk == c, wide[64 * c : 64 * c + 64], chosen)
        picked[j] = chosen.astype(BF16)
        tsum[...] += wts[j] * chosen

    each(16, gather, 2)

    total = tsum[...]
    act = (total * sigmoid(total)).astype(BF16)
    dt[...] = dsum[...] * silu_grad(total)
    up_grad = dot(act, cot[...])
    for s in range(16):
        own_u[s] = up_grad[8 * (s // 2) : 8 * (s // 2) + 8, 256 * (s % 2) : 256 * (s % 2) + 256]
    sems_u = [(sem_u.at[0, t], sem_u.at[1, t]) for t in range(3)]
    scatter_u, middle_u, spread_u, final_u, gather_u = small_stages(own_u, got_u, mid_u, last_u, sems_u)
    scatter_u.start()

    table_sum[...] = jnp.zeros_like(table_sum)

    def scatter(j):
        chunk = jnp.right_shift(index[pl.ds(j, 1), :], 8)
        slope = dt[...]
        term = (slope * wts[j]).astype(BF16)
        picked[j] = (slope * picked[j].astype(F32)).astype(BF16)
        parts = [term * jnp.where(chunk == c, 1.0, 0.0).astype(BF16) for c in range(6)]
        table_sum[...] += dot(jnp.concatenate(parts, axis=0), hot[j], 1, 1)

    each(8, scatter, 2)
    res_scatter.arrived()
    mine_far = pl.ds(pl.multiple_of(16 * far, 16), 16)
    part = res_sum[pl.ds(pl.multiple_of(mine + 16 * far, 16), 16), :] + half_got[mine_far, :].astype(F32)
    for s in range(15):
        part = part + far_got[s].astype(F32)
    res_mid[z] = part.astype(BF16)
    res_spread = Exchange(7, lambda s: res_mid.at[z], lambda s: res_mid.at[z], res_mid.at[0:7], res_mid.at[0:7], (sem_z.at[0], sem_z.at[1]), z_peer)
    res_spread.start()
    each(8, lambda j: scatter(j + 8), 2)

    def back_copy(k):
        return remote(back_send.at[k], back_got.at[k], sem_back.at[0], sem_back.at[1], behind[k])

    for k in range(4):
        back_send[k] = table_sum[256 + 64 * (k // 2) : 320 + 64 * (k // 2), 128 * (k % 2) : 128 * (k % 2) + 128].astype(BF16)
        back_copy(k).start()

    basis_grad = jnp.zeros((16, 64), F32)
    for j in range(16):
        basis_grad = basis_grad + dot(basis[16 * j : 16 * j + 16, :], picked[j], 1, 1)
    basis_got[near] = basis_grad
    basis_a = Exchange(15, lambda s: basis_got.at[near], lambda s: basis_got.at[near], basis_got.at[0:15], basis_got.at[0:15], (sem_basis.at[0, 0], sem_basis.at[1, 0]), near_peer)
    basis_a.start()

    middle_u()
    spread_u.start()
    res_spread.arrived()
    part = res_mid[0].astype(F32)
    for s in range(1, 8):
        part = part + res_mid[s].astype(F32)
    res_last[mine_far, :] = part.astype(BF16)
    res_gather = Exchange(
        15, lambda s: res_last.at[mine_far, :], lambda s: res_last.at[mine_far, :], res_last.at[0:240], res_last.at[0:240], (sem_far.at[0, 1], sem_far.at[1, 1]), far_peer
    )
    res_gather.start()

    pltpu.make_async_copy(back_got, back_got, sem_back.at[1]).wait()
    returned = table_sum[0:256, :]
    for k in range(4):
        chunk = jnp.right_shift(rows_out[k : k + 1, :], 8)
        term = back_got[k]
        parts = [term * jnp.where(chunk == c, 1.0, 0.0).astype(BF16) for c in range(4)]
        returned = returned + dot(jnp.concatenate(parts, axis=0), ghost_hot[:, 128 * k : 128 * k + 128], 1, 1)
    returned = (returned * silu_grad(pre[...])).astype(BF16)
    for c in range(4):
        dpre[:, 256 * c : 256 * c + 256] = returned[64 * c : 64 * c + 64, :]
    down_grad = dot(dpre[...], embed[...])
    for s in range(16):
        own_d[s] = down_grad[8 * (s // 2) : 8 * (s // 2) + 8, 256 * (s % 2) : 256 * (s % 2) + 256]
    sems_d = [(sem_d.at[0, t], sem_d.at[1, t]) for t in range(3)]
    scatter_d, middle_d, spread_d, final_d, gather_d = small_stages(own_d, got_d, mid_d, last_d, sems_d)
    scatter_d.start()

    def edge(i):
        rows = pl.ds(pl.multiple_of(256 * i, 256), 256)
        value = dot(dres[rows, :], w_res[...], 1, 1) + dot(dpre[:, rows], down_t[...], 0, 0)
        edge_out[rows, :] = value.astype(BF16)

    each(4, edge)
    edge_copy = pltpu.make_async_copy(edge_out, edge_hbm, sem_out.at[0])
    edge_copy.start()

    basis_a.arrived()
    basis_total = basis_got[0]
    for s in range(1, 16):
        basis_total = basis_total + basis_got[s]
    basis_mid[far] = basis_total
    basis_b = Exchange(15, lambda s: basis_mid.at[far], lambda s: basis_mid.at[far], basis_mid.at[0:15], basis_mid.at[0:15], (sem_basis.at[0, 1], sem_basis.at[1, 1]), far_peer)
    basis_b.start()

    middle_d()
    spread_d.start()
    final_u()
    gather_u.start()
    res_gather.arrived()
    core_last = remote(res_last, res_other, sem_core.at[2], sem_core.at[3], core_peer())
    core_last.start()
    res_out[pl.ds(mine, 256), :] = res_last[...]
    final_d()
    gather_d.start()
    basis_b.arrived()
    basis_total = basis_mid[0]
    for s in range(1, 16):
        basis_total = basis_total + basis_mid[s]
    small_out[128:144, 0:64] = basis_total
    gather_u.arrived()
    for s in range(16):
        small_out[64 + 8 * (s // 2) : 72 + 8 * (s // 2), 256 * (s % 2) : 256 * (s % 2) + 256] = last_u[s].astype(F32)
    core_last.wait_recv()
    res_out[other_half, :] = res_other[...]
    res_copy = pltpu.make_async_copy(res_out, res_hbm, sem_out.at[1])
    res_copy.start()
    pltpu.make_async_copy(ghost_send, ghost_send, sem_ghost.at[0]).wait()
    pltpu.make_async_copy(back_send, back_send, sem_back.at[0]).wait()
    for exchange in (scatter_u, spread_u, gather_u, scatter_d, spread_d, basis_a, basis_b, res_scatter, res_spread, res_gather):
        exchange.sent()
    core_first.wait_send()
    core_last.wait_send()
    gather_d.arrived()
    for s in range(16):
        small_out[8 * (s // 2) : 8 * (s // 2) + 8, 256 * (s % 2) : 256 * (s % 2) + 256] = last_d[s].astype(F32)
    gather_d.sent()
    edge_copy.wait()
    res_copy.wait()


def copy_kernel(edge, res, small, edge_out, res_out, down_out, up_out, basis_out):
    edge_out[...] = edge[...]
    res_out[...] = res[...].astype(F32)
    down_out[...] = small[0:64, :]
    up_out[...] = small[64:128, :]
    basis_out[...] = small[128:144, 0:64]


def hand_over(edge, res, small):
    shapes = (((1024, 512), BF16), ((512, 512), F32), ((64, 512), F32), ((64, 512), F32), ((16, 64), F32))
    return pl.pallas_call(
        copy_kernel,
        out_shape=tuple(jax.ShapeDtypeStruct(*shape) for shape in shapes),
        in_specs=[pl.BlockSpec(memory_space=pltpu.VMEM)] * 3,
        out_specs=[pl.BlockSpec(memory_space=pltpu.VMEM)] * 5,
        compiler_params=pltpu.CompilerParams(vmem_limit_bytes=8 * 1024 * 1024),
        name="hand_over",
    )(edge, res, small)


def shards(
    embed, cotangent, basis, triplet_row_index, triplet_slot_count, outgoing_edge_rows,
    residual_weight, down_weight, up_weight, basis_weight,
):
    vmem = pltpu.VMEM
    edge, res, small = pl.pallas_call(
        fused_kernel,
        out_shape=(
            vmem((1024, 512), BF16),
            vmem((512, 512), BF16),
            vmem((144, 512), F32),
        ),
        in_specs=[pl.BlockSpec(memory_space=pltpu.HBM)] * 10,
        out_specs=[pl.BlockSpec(memory_space=pl.ANY), pl.BlockSpec(memory_space=pl.ANY), pl.BlockSpec(memory_space=vmem)],
        scratch_shapes=[
            vmem((1024, 512), BF16),
            vmem((1024, 512), BF16),
            vmem((256, 1024), BF16),
            vmem((16, 1024), jnp.int32),
            vmem((1, 1024), jnp.int32),
            vmem((4, 128), jnp.int32),
            vmem((512, 512), BF16),
            vmem((64, 512), BF16),
            vmem((64, 512), BF16),
            vmem((16, 64), BF16),
            vmem((384, 256), BF16),
            vmem((256, 256), F32),
            vmem((4, 64, 128), BF16),
            vmem((256, 512), BF16),
            vmem((1024, 512), BF16),
            vmem((512, 512), F32),
            vmem((16, 64, 1024), F32),
            vmem((64, 1024), F32),
            vmem((16, 256, 1024), BF16),
            vmem((16, 64, 1024), BF16),
            vmem((64, 1024), F32),
            vmem((64, 1024), F32),
            vmem((384, 256), F32),
            vmem((4, 64, 128), BF16),
            vmem((4, 64, 128), BF16),
            vmem((64, 1024), BF16),
            vmem((16, 8, 256), F32),
            vmem((15, 8, 256), F32),
            vmem((16, 8, 256), F32),
            vmem((16, 8, 256), BF16),
            vmem((16, 8, 256), F32),
            vmem((15, 8, 256), F32),
            vmem((16, 8, 256), F32),
            vmem((16, 8, 256), BF16),
            vmem((16, 16, 64), F32),
            vmem((16, 16, 64), F32),
            vmem((256, 512), BF16),
            vmem((256, 512), BF16),
            vmem((16, 16, 512), BF16),
            vmem((15, 16, 512), BF16),
            vmem((8, 16, 512), BF16),
            vmem((256, 512), BF16),
            vmem((256, 512), BF16),
            DMA((2,)),
            DMA((2,)),
            DMA((2, 3)),
            DMA((2, 3)),
            DMA((2, 2)),
            DMA((4,)),
            DMA((2,)),
            DMA((2, 2)),
            DMA((10,)),
            DMA((2,)),
            vmem((1024, 512), BF16),
            vmem((512, 512), BF16),
        ],
        compiler_params=pltpu.CompilerParams(
            collective_id=0, has_side_effects=True, vmem_limit_bytes=40 * 1024 * 1024
        ),
        name="fused",
    )(
        *(
            pltpu.with_memory_space_constraint(value, pltpu.HBM)
            for value in (
                embed, cotangent, basis.reshape(256, 1024), triplet_row_index, triplet_slot_count.reshape(1, 1024),
                outgoing_edge_rows, residual_weight, down_weight.T, up_weight, basis_weight,
            )
        )
    )
    edge, res, down, up, base = hand_over(edge, res, small)
    return edge, res, down.T, up, base


def solution(mesh):
    in_specs = (
        P(("slab", "brick"), None),
        P(("slab", "brick"), None),
        P(None, None, ("slab", "brick")),
        P(None, ("slab", "brick")),
        P(("slab", "brick")),
        P(None, ("slab", "brick")),
        P(),
        P(),
        P(),
        P(),
    )
    out_specs = (P(("slab", "brick"), None), P(), P(), P(), P())
    return jax.shard_map(shards, mesh=mesh, in_specs=in_specs, out_specs=out_specs, check_vma=False)
```

```python
import functools

import jax
import jax.numpy as jnp
from jax import lax
from jax.experimental import pallas as pl
from jax.experimental.pallas import tpu as pltpu
from jax.sharding import PartitionSpec as P

MESH = pl.DeviceIdType.MESH
DMA = pltpu.SemaphoreType.DMA


def where_am_i():
    slab, brick = lax.axis_index("slab"), lax.axis_index("brick")
    near = lax.rem(brick, 16)
    far = slab * 2 + brick // 16
    return slab, brick, near, far


def near_peer(step):
    slab, brick, near, _ = where_am_i()
    return slab, (brick // 16) * 16 + lax.rem(near + step, 16)


def far_peer(step):
    _, _, near, far = where_am_i()
    other = lax.rem(far + step, 16)
    return other // 2, lax.rem(other, 2) * 16 + near


def z_peer(step):
    slab, brick, near, _ = where_am_i()
    return slab, (brick // 16) * 16 + lax.rem(near + 2 * step, 16)


def core_peer():
    slab, brick, _, _ = where_am_i()
    return slab, brick + 1 - 2 * lax.rem(brick, 2)


def remote(source, target, send, recv, peer):
    return pltpu.make_async_remote_copy(
        src_ref=source, dst_ref=target, send_sem=send, recv_sem=recv,
        device_id=peer, device_id_type=MESH,
    )


def each(count, body, unroll=1):
    def step(index, carry):
        body(index)
        return carry

    lax.fori_loop(0, count, step, 0, unroll=unroll)


class Exchange:
    def __init__(self, count, source, target, gone, came, sems, peer):
        self.count, self.source, self.target, self.gone, self.came = count, source, target, gone, came
        self.sems, self.peer = sems, peer

    def start(self):
        send, recv = self.sems
        each(self.count, lambda s: remote(self.source(s), self.target(s), send, recv, self.peer(s + 1)).start())

    def arrived(self):
        pltpu.make_async_copy(self.came, self.came, self.sems[1]).wait()

    def sent(self):
        pltpu.make_async_copy(self.gone, self.gone, self.sems[0]).wait()


def small_stages(own, got, mid, last, sems):
    _, _, near, far = where_am_i()
    scatter = Exchange(
        15, lambda s: own.at[lax.rem(far + s + 1, 16)], lambda s: got.at[s], got, got, sems[0], far_peer
    )
    spread = Exchange(15, lambda s: mid.at[near], lambda s: mid.at[near], mid.at[0:15], mid.at[0:15], sems[1], near_peer)
    gather = Exchange(15, lambda s: last.at[far], lambda s: last.at[far], last.at[0:15], last.at[0:15], sems[2], far_peer)

    def middle():
        scatter.arrived()
        total = own[far]
        for s in range(15):
            total = total + got[s]
        mid[near] = total.astype(mid.dtype)

    def final():
        spread.arrived()
        total = mid[0].astype(F32)
        for s in range(1, 16):
            total = total + mid[s].astype(F32)
        last[far] = total.astype(last.dtype)

    return scatter, middle, spread, final, gather


def announce():
    slab, brick, _, _ = where_am_i()
    barrier = pltpu.get_barrier_semaphore()

    def tell(peer):
        pl.semaphore_signal(barrier, inc=1, device_id=peer, device_id_type=MESH)

    each(15, lambda s: tell(near_peer(s + 1)))
    each(15, lambda s: tell(far_peer(s + 1)))
    tell((slab, lax.rem(brick + 1, 32)))
    tell((slab, lax.rem(brick + 31, 32)))
    return barrier


F32, BF16 = jnp.float32, jnp.bfloat16


def sigmoid(value):
    return 0.5 * jnp.tanh(0.5 * value) + 0.5


def silu_grad(value):
    sig = sigmoid(value)
    return sig * (1.0 + value * (1.0 - sig))


def dot(a, b, ca=1, cb=0):
    return lax.dot_general(a, b, (((ca,), (cb,)), ((), ())), preferred_element_type=F32)


def low_onehot(low):
    width = low.shape[1]
    positions = lax.broadcasted_iota(jnp.int32, (256, width), 0).astype(F32).astype(BF16)
    return jnp.where(positions == low.astype(F32).astype(BF16), jnp.ones((), BF16), jnp.zeros((), BF16))


def slice_of(s):
    return pl.ds(8 * (s // 2), 8), pl.ds(256 * (s % 2), 256)


def fused_kernel(
    embed_hbm, cot_hbm, basis_hbm, index_hbm, count_hbm, rows_hbm, w_res_hbm, down_hbm, w_up_hbm, w_basis_hbm,
    edge_hbm, res_hbm, small_out,
    embed, cot, basis, index, count, rows_out, w_res, down_t, w_up, w_basis,
    w_block, terms, ghost_sum,
    table, pre, ghost_send, ghost_hot, dres, res_sum, wts, dsum,
    hot, picked, tsum, dt, table_sum, back_send, back_got, dpre,
    own_d, got_d, mid_d, last_d, own_u, got_u, mid_u, last_u, basis_got, basis_mid,
    half_send, half_got, far_send, far_got, res_mid, res_last, res_other,
    sem_ghost, sem_back, sem_d, sem_u, sem_basis, sem_core, sem_z, sem_far, sem_in, sem_out, edge_out, res_out,
):
    slab, brick, near, far = where_am_i()
    core, z = lax.rem(near, 2), near // 2
    ahead = ((lax.rem(slab + 1, 8), brick), (lax.rem(slab + 7, 8), brick),
             (slab, lax.rem(brick + 1, 32)), (slab, lax.rem(brick + 31, 32)))
    behind = (ahead[1], ahead[0], ahead[3], ahead[2])
    loads = {}
    for place, (name, source, target) in enumerate((
        ("down", down_hbm, down_t), ("rows", rows_hbm, rows_out), ("w_res", w_res_hbm, w_res),
        ("cot", cot_hbm, cot), ("basis", basis_hbm, basis), ("w_basis", w_basis_hbm, w_basis), ("w_up", w_up_hbm, w_up),
        ("index", index_hbm, index), ("count", count_hbm, count),
    )):
        loads[name] = pltpu.make_async_copy(source, target, sem_in.at[place])
    quarters = [
        pltpu.make_async_copy(embed_hbm.at[256 * c : 256 * c + 256, :], embed.at[256 * c : 256 * c + 256, :], sem_in.at[9 + c])
        for c in range(4)
    ]
    loads["down"].start()
    for quarter in quarters:
        quarter.start()
    loads["rows"].start()
    barrier = announce()
    for name in ("w_res", "cot", "basis", "w_basis", "w_up", "index", "count"):
        loads[name].start()

    loads["down"].wait()
    for c in range(4):
        quarters[c].wait()
        part = dot(down_t[...], embed[256 * c : 256 * c + 256, :], 1, 1)
        pre[64 * c : 64 * c + 64, :] = part
        table[64 * c : 64 * c + 64, :] = (part * sigmoid(part)).astype(BF16)
    loads["rows"].wait()
    for k in range(4):
        sent = rows_out[k : k + 1, :]
        lanes = pl.ds(128 * k, 128)
        ghost_hot[:, lanes] = low_onehot(jnp.bitwise_and(sent, 255))
        wide = dot(table[0:256, :], ghost_hot[:, lanes])
        chunk = jnp.right_shift(sent, 8)
        chosen = wide[0:64]
        for c in range(1, 4):
            chosen = jnp.where(chunk == c, wide[64 * c : 64 * c + 64], chosen)
        ghost_send[k] = chosen.astype(BF16)
    loads["w_res"].wait()
    loads["cot"].wait()

    def residual(i):
        rows = pl.ds(pl.multiple_of(256 * i, 256), 256)
        value = dot(embed[rows, :], w_res[...])
        dres[rows, :] = (cot[rows, :].astype(F32) * silu_grad(value)).astype(BF16)

    each(4, residual, 2)

    pl.semaphore_wait(barrier, 32)

    def ghost_copy(k):
        place = table.at[pl.ds(256 + 64 * (k // 2), 64), pl.ds(128 * (k % 2), 128)]
        return remote(ghost_send.at[k], place, sem_ghost.at[0], sem_ghost.at[1], ahead[k])

    for k in range(4):
        ghost_copy(k).start()

    def residual_grad(i):
        rows = pl.ds(pl.multiple_of(128 * i, 128), 128)
        res_sum[rows, :] = dot(embed[:, rows], dres[...], 0, 0)

    each(4, residual_grad, 2)
    other_half = pl.ds(pl.multiple_of((1 - core) * 256, 256), 256)
    half_send[...] = res_sum[other_half, :].astype(BF16)
    core_first = remote(half_send, half_got, sem_core.at[0], sem_core.at[1], core_peer())
    core_first.start()

    for name in ("basis", "w_basis", "w_up", "index", "count"):
        loads[name].wait()
    spread_n = (lax.broadcasted_iota(jnp.int32, (16, 256), 1) % 16) == lax.broadcasted_iota(jnp.int32, (16, 256), 0)
    wide_w = dot(w_basis[...], jnp.where(spread_n, 1.0, 0.0).astype(BF16), 0, 0)
    lane_slot = lax.broadcasted_iota(jnp.int32, (64, 256), 1) // 16
    for j in range(16):
        w_block[64 * j : 64 * j + 64, :] = jnp.where(lane_slot == j, wide_w, 0.0).astype(BF16)

    def slot_weights(i):
        lanes = pl.ds(pl.multiple_of(256 * i, 256), 256)
        wts[:, lanes] = dot(w_block[...], basis[:, lanes])

    each(4, slot_weights, 2)
    dsum[...] = dot(w_up[...], cot[...], 1, 1)

    core_first.wait_recv()
    mine = pl.multiple_of(core * 256, 256)

    def to_far(t):
        rows = pl.ds(pl.multiple_of(mine + 16 * t, 16), 16)
        got = half_got[pl.ds(pl.multiple_of(16 * t, 16), 16), :]
        far_send[t] = (res_sum[rows, :] + got.astype(F32)).astype(BF16)

    each(16, to_far)
    res_scatter = Exchange(
        15, lambda s: far_send.at[lax.rem(far + s + 1, 16)], lambda s: far_got.at[s], far_got, far_got, (sem_far.at[0, 0], sem_far.at[1, 0]), far_peer
    )
    res_scatter.start()
    pltpu.make_async_copy(ghost_send, ghost_send, sem_ghost.at[1]).wait()
    tsum[...] = jnp.zeros_like(tsum)

    def gather(j):
        row = index[pl.ds(j, 1), :]
        low = jnp.where(j < count[...], jnp.bitwise_and(row, 255), -1)
        chunk = jnp.right_shift(row, 8)
        hot[j] = low_onehot(low)
        wide = dot(table[...], hot[j])
        chosen = wide[0:64]
        for c in range(1, 6):
            chosen = jnp.where(chunk == c, wide[64 * c : 64 * c + 64], chosen)
        picked[j] = chosen.astype(BF16)
        tsum[...] += wts[pl.ds(pl.multiple_of(64 * j, 64), 64), :] * chosen

    each(16, gather, 2)

    total = tsum[...]
    act = (total * sigmoid(total)).astype(BF16)
    dt[...] = dsum[...] * silu_grad(total)
    up_grad = dot(act, cot[...])
    for s in range(16):
        own_u[s] = up_grad[8 * (s // 2) : 8 * (s // 2) + 8, 256 * (s % 2) : 256 * (s % 2) + 256]
    sems_u = [(sem_u.at[0, t], sem_u.at[1, t]) for t in range(3)]
    scatter_u, middle_u, spread_u, final_u, gather_u = small_stages(own_u, got_u, mid_u, last_u, sems_u)
    scatter_u.start()

    ghost_sum[...] = jnp.zeros_like(ghost_sum)
    table_sum[...] = jnp.zeros_like(table_sum)

    def only(chunk, c):
        return jnp.where(chunk == c, 1.0, 0.0).astype(BF16)

    def scatter_ghosts(j):
        chunk = jnp.right_shift(index[pl.ds(j, 1), :], 8)
        slope = dt[...]
        term = (slope * wts[pl.ds(pl.multiple_of(64 * j, 64), 64), :]).astype(BF16)
        terms[j] = term
        picked[j] = (slope * picked[j].astype(F32)).astype(BF16)
        parts = [term * only(chunk, c) for c in (4, 5)]
        ghost_sum[...] += dot(hot[j], jnp.concatenate(parts, axis=0), 1, 1)

    each(16, scatter_ghosts, 2)

    def back_copy(k):
        return remote(back_send.at[k], back_got.at[k], sem_back.at[0], sem_back.at[1], behind[k])

    ghost_rows = ghost_sum[...].T
    for k in range(4):
        back_send[k] = ghost_rows[64 * (k // 2) : 64 * (k // 2) + 64, 128 * (k % 2) : 128 * (k % 2) + 128].astype(BF16)
        back_copy(k).start()

    res_scatter.arrived()
    mine_far = pl.ds(pl.multiple_of(16 * far, 16), 16)
    part = res_sum[pl.ds(pl.multiple_of(mine + 16 * far, 16), 16), :] + half_got[mine_far, :].astype(F32)
    for s in range(15):
        part = part + far_got[s].astype(F32)
    res_mid[z] = part.astype(BF16)
    res_spread = Exchange(7, lambda s: res_mid.at[z], lambda s: res_mid.at[z], res_mid.at[0:7], res_mid.at[0:7], (sem_z.at[0], sem_z.at[1]), z_peer)
    res_spread.start()
    middle_u()
    spread_u.start()
    def scatter_own(j):
        chunk = jnp.right_shift(index[pl.ds(j, 1), :], 8)
        parts = [terms[j] * only(chunk, c) for c in range(4)]
        table_sum[...] += dot(jnp.concatenate(parts, axis=0), hot[j], 1, 1)

    each(16, scatter_own, 2)
    pltpu.make_async_copy(back_got, back_got, sem_back.at[1]).wait()
    returned = table_sum[...]
    for k in range(4):
        chunk = jnp.right_shift(rows_out[k : k + 1, :], 8)
        term = back_got[k]
        parts = [term * jnp.where(chunk == c, 1.0, 0.0).astype(BF16) for c in range(4)]
        returned = returned + dot(jnp.concatenate(parts, axis=0), ghost_hot[:, 128 * k : 128 * k + 128], 1, 1)
    returned = (returned * silu_grad(pre[...])).astype(BF16)
    for c in range(4):
        dpre[:, 256 * c : 256 * c + 256] = returned[64 * c : 64 * c + 64, :]
    down_grad = dot(dpre[...], embed[...])
    for s in range(16):
        own_d[s] = down_grad[8 * (s // 2) : 8 * (s // 2) + 8, 256 * (s % 2) : 256 * (s % 2) + 256]
    sems_d = [(sem_d.at[0, t], sem_d.at[1, t]) for t in range(3)]
    scatter_d, middle_d, spread_d, final_d, gather_d = small_stages(own_d, got_d, mid_d, last_d, sems_d)
    scatter_d.start()

    basis_grad = jnp.zeros((16, 64), F32)
    for j in range(16):
        basis_grad = basis_grad + dot(basis[16 * j : 16 * j + 16, :], picked[j], 1, 1)
    basis_got[near] = basis_grad
    basis_a = Exchange(15, lambda s: basis_got.at[near], lambda s: basis_got.at[near], basis_got.at[0:15], basis_got.at[0:15], (sem_basis.at[0, 0], sem_basis.at[1, 0]), near_peer)
    basis_a.start()

    def edge(i):
        rows = pl.ds(pl.multiple_of(256 * i, 256), 256)
        value = dot(dres[rows, :], w_res[...], 1, 1) + dot(dpre[:, rows], down_t[...], 0, 0)
        edge_out[rows, :] = value.astype(BF16)

    each(4, edge, 2)
    edge_copy = pltpu.make_async_copy(edge_out, edge_hbm, sem_out.at[0])
    edge_copy.start()

    middle_d()
    spread_d.start()
    res_spread.arrived()
    part = res_mid[0].astype(F32)
    for s in range(1, 8):
        part = part + res_mid[s].astype(F32)
    res_last[mine_far, :] = part.astype(BF16)
    res_gather = Exchange(
        15, lambda s: res_last.at[mine_far, :], lambda s: res_last.at[mine_far, :], res_last.at[0:240], res_last.at[0:240], (sem_far.at[0, 1], sem_far.at[1, 1]), far_peer
    )
    res_gather.start()

    final_u()
    gather_u.start()
    basis_a.arrived()
    basis_total = basis_got[0]
    for s in range(1, 16):
        basis_total = basis_total + basis_got[s]
    basis_mid[far] = basis_total
    basis_b = Exchange(15, lambda s: basis_mid.at[far], lambda s: basis_mid.at[far], basis_mid.at[0:15], basis_mid.at[0:15], (sem_basis.at[0, 1], sem_basis.at[1, 1]), far_peer)
    basis_b.start()

    final_d()
    gather_d.start()
    res_gather.arrived()
    core_last = remote(res_last, res_other, sem_core.at[2], sem_core.at[3], core_peer())
    core_last.start()
    res_out[pl.ds(mine, 256), :] = res_last[...]
    basis_b.arrived()
    basis_total = basis_mid[0]
    for s in range(1, 16):
        basis_total = basis_total + basis_mid[s]
    small_out[128:144, 0:64] = basis_total
    gather_u.arrived()
    for s in range(16):
        small_out[64 + 8 * (s // 2) : 72 + 8 * (s // 2), 256 * (s % 2) : 256 * (s % 2) + 256] = last_u[s].astype(F32)
    core_last.wait_recv()
    res_out[other_half, :] = res_other[...]
    res_copy = pltpu.make_async_copy(res_out, res_hbm, sem_out.at[1])
    res_copy.start()
    pltpu.make_async_copy(ghost_send, ghost_send, sem_ghost.at[0]).wait()
    pltpu.make_async_copy(back_send, back_send, sem_back.at[0]).wait()
    for exchange in (scatter_u, spread_u, gather_u, scatter_d, spread_d, basis_a, basis_b, res_scatter, res_spread, res_gather):
        exchange.sent()
    core_first.wait_send()
    core_last.wait_send()
    gather_d.arrived()
    for s in range(16):
        small_out[8 * (s // 2) : 8 * (s // 2) + 8, 256 * (s % 2) : 256 * (s % 2) + 256] = last_d[s].astype(F32)
    gather_d.sent()
    edge_copy.wait()
    res_copy.wait()


def copy_kernel(edge, res, small, edge_out, res_out, down_out, up_out, basis_out):
    edge_out[...] = edge[...]
    res_out[...] = res[...].astype(F32)
    down_out[...] = small[0:64, :]
    up_out[...] = small[64:128, :]
    basis_out[...] = small[128:144, 0:64]


def hand_over(edge, res, small):
    shapes = (((1024, 512), BF16), ((512, 512), F32), ((64, 512), F32), ((64, 512), F32), ((16, 64), F32))
    return pl.pallas_call(
        copy_kernel,
        out_shape=tuple(jax.ShapeDtypeStruct(*shape) for shape in shapes),
        in_specs=[pl.BlockSpec(memory_space=pltpu.VMEM)] * 3,
        out_specs=[pl.BlockSpec(memory_space=pltpu.VMEM)] * 5,
        compiler_params=pltpu.CompilerParams(vmem_limit_bytes=8 * 1024 * 1024),
        name="hand_over",
    )(edge, res, small)


def shards(
    embed, cotangent, basis, triplet_row_index, triplet_slot_count, outgoing_edge_rows,
    residual_weight, down_weight, up_weight, basis_weight,
):
    vmem = pltpu.VMEM
    edge, res, small = pl.pallas_call(
        fused_kernel,
        out_shape=(
            vmem((1024, 512), BF16),
            vmem((512, 512), BF16),
            vmem((144, 512), F32),
        ),
        in_specs=[pl.BlockSpec(memory_space=pltpu.HBM)] * 10,
        out_specs=[pl.BlockSpec(memory_space=pl.ANY), pl.BlockSpec(memory_space=pl.ANY), pl.BlockSpec(memory_space=vmem)],
        scratch_shapes=[
            vmem((1024, 512), BF16),
            vmem((1024, 512), BF16),
            vmem((256, 1024), BF16),
            vmem((16, 1024), jnp.int32),
            vmem((1, 1024), jnp.int32),
            vmem((4, 128), jnp.int32),
            vmem((512, 512), BF16),
            vmem((64, 512), BF16),
            vmem((64, 512), BF16),
            vmem((16, 64), BF16),
            vmem((1024, 256), BF16),
            vmem((16, 64, 1024), BF16),
            vmem((256, 128), F32),
            vmem((384, 256), BF16),
            vmem((256, 256), F32),
            vmem((4, 64, 128), BF16),
            vmem((256, 512), BF16),
            vmem((1024, 512), BF16),
            vmem((512, 512), F32),
            vmem((1024, 1024), F32),
            vmem((64, 1024), F32),
            vmem((16, 256, 1024), BF16),
            vmem((16, 64, 1024), BF16),
            vmem((64, 1024), F32),
            vmem((64, 1024), F32),
            vmem((256, 256), F32),
            vmem((4, 64, 128), BF16),
            vmem((4, 64, 128), BF16),
            vmem((64, 1024), BF16),
            vmem((16, 8, 256), F32),
            vmem((15, 8, 256), F32),
            vmem((16, 8, 256), BF16),
            vmem((16, 8, 256), BF16),
            vmem((16, 8, 256), F32),
            vmem((15, 8, 256), F32),
            vmem((16, 8, 256), BF16),
            vmem((16, 8, 256), BF16),
            vmem((16, 16, 64), F32),
            vmem((16, 16, 64), F32),
            vmem((256, 512), BF16),
            vmem((256, 512), BF16),
            vmem((16, 16, 512), BF16),
            vmem((15, 16, 512), BF16),
            vmem((8, 16, 512), BF16),
            vmem((256, 512), BF16),
            vmem((256, 512), BF16),
            DMA((2,)),
            DMA((2,)),
            DMA((2, 3)),
            DMA((2, 3)),
            DMA((2, 2)),
            DMA((4,)),
            DMA((2,)),
            DMA((2, 2)),
            DMA((13,)),
            DMA((2,)),
            vmem((1024, 512), BF16),
            vmem((512, 512), BF16),
        ],
        compiler_params=pltpu.CompilerParams(
            collective_id=0, has_side_effects=True, vmem_limit_bytes=40 * 1024 * 1024
        ),
        name="fused",
    )(
        *(
            pltpu.with_memory_space_constraint(value, pltpu.HBM)
            for value in (
                embed, cotangent, basis.reshape(256, 1024), triplet_row_index, triplet_slot_count.reshape(1, 1024),
                outgoing_edge_rows, residual_weight, down_weight.T, up_weight, basis_weight,
            )
        )
    )
    edge, res, down, up, base = hand_over(edge, res, small)
    return edge, res, down.T, up, base


def solution(mesh):
    in_specs = (
        P(("slab", "brick"), None),
        P(("slab", "brick"), None),
        P(None, None, ("slab", "brick")),
        P(None, ("slab", "brick")),
        P(("slab", "brick")),
        P(None, ("slab", "brick")),
        P(),
        P(),
        P(),
        P(),
    )
    out_specs = (P(("slab", "brick"), None), P(), P(), P(), P())
    return jax.shard_map(shards, mesh=mesh, in_specs=in_specs, out_specs=out_specs, check_vma=False)
```

```python
import functools

import jax
import jax.numpy as jnp
from jax import lax
from jax.experimental import pallas as pl
from jax.experimental.pallas import tpu as pltpu
from jax.sharding import PartitionSpec as P

MESH = pl.DeviceIdType.MESH
DMA = pltpu.SemaphoreType.DMA


def where_am_i():
    slab, brick = lax.axis_index("slab"), lax.axis_index("brick")
    near = lax.rem(brick, 16)
    far = slab * 2 + brick // 16
    return slab, brick, near, far


def near_peer(step):
    slab, brick, near, _ = where_am_i()
    return slab, (brick // 16) * 16 + lax.rem(near + step, 16)


def far_peer(step):
    _, _, near, far = where_am_i()
    other = lax.rem(far + step, 16)
    return other // 2, lax.rem(other, 2) * 16 + near


def z_peer(step):
    slab, brick, near, _ = where_am_i()
    return slab, (brick // 16) * 16 + lax.rem(near + 2 * step, 16)


def core_peer():
    slab, brick, _, _ = where_am_i()
    return slab, brick + 1 - 2 * lax.rem(brick, 2)


def remote(source, target, send, recv, peer):
    return pltpu.make_async_remote_copy(
        src_ref=source, dst_ref=target, send_sem=send, recv_sem=recv,
        device_id=peer, device_id_type=MESH,
    )


def each(count, body, unroll=1):
    def step(index, carry):
        body(index)
        return carry

    lax.fori_loop(0, count, step, 0, unroll=unroll)


class Exchange:
    def __init__(self, count, source, target, gone, came, sems, peer):
        self.count, self.source, self.target, self.gone, self.came = count, source, target, gone, came
        self.sems, self.peer = sems, peer

    def start(self):
        send, recv = self.sems
        each(self.count, lambda s: remote(self.source(s), self.target(s), send, recv, self.peer(s + 1)).start())

    def arrived(self):
        pltpu.make_async_copy(self.came, self.came, self.sems[1]).wait()

    def sent(self):
        pltpu.make_async_copy(self.gone, self.gone, self.sems[0]).wait()


def small_stages(own, got, mid, last, sems):
    _, _, near, far = where_am_i()
    scatter = Exchange(
        15, lambda s: own.at[lax.rem(far + s + 1, 16)], lambda s: got.at[s], got, got, sems[0], far_peer
    )
    spread = Exchange(15, lambda s: mid.at[near], lambda s: mid.at[near], mid.at[0:15], mid.at[0:15], sems[1], near_peer)
    gather = Exchange(15, lambda s: last.at[far], lambda s: last.at[far], last.at[0:15], last.at[0:15], sems[2], far_peer)

    def middle():
        scatter.arrived()
        total = own[far]
        for s in range(15):
            total = total + got[s]
        mid[near] = total.astype(mid.dtype)

    def final():
        spread.arrived()
        total = mid[0].astype(F32)
        for s in range(1, 16):
            total = total + mid[s].astype(F32)
        last[far] = total.astype(last.dtype)

    return scatter, middle, spread, final, gather


def announce():
    slab, brick, _, _ = where_am_i()
    barrier = pltpu.get_barrier_semaphore()

    def tell(peer):
        pl.semaphore_signal(barrier, inc=1, device_id=peer, device_id_type=MESH)

    each(15, lambda s: tell(near_peer(s + 1)))
    each(15, lambda s: tell(far_peer(s + 1)))
    tell((slab, lax.rem(brick + 1, 32)))
    tell((slab, lax.rem(brick + 31, 32)))
    return barrier


F32, BF16 = jnp.float32, jnp.bfloat16


def sigmoid(value):
    return 0.5 * jnp.tanh(0.5 * value) + 0.5


def silu_grad(value):
    sig = sigmoid(value)
    return sig * (1.0 + value * (1.0 - sig))


def dot(a, b, ca=1, cb=0):
    return lax.dot_general(a, b, (((ca,), (cb,)), ((), ())), preferred_element_type=F32)


def low_onehot(low):
    width = low.shape[1]
    positions = lax.broadcasted_iota(jnp.int32, (256, width), 0).astype(F32).astype(BF16)
    return jnp.where(positions == low.astype(F32).astype(BF16), jnp.ones((), BF16), jnp.zeros((), BF16))


def slice_of(s):
    return pl.ds(8 * (s // 2), 8), pl.ds(256 * (s % 2), 256)


def fused_kernel(
    embed_hbm, cot_hbm, basis_hbm, index_hbm, count_hbm, rows_hbm, w_res_hbm, down_hbm, w_up_hbm, w_basis_hbm,
    edge_hbm, res_hbm, small_out, basis_dest,
    embed, cot, basis, index, count, rows_out, w_res, down_t, w_up, w_basis,
    terms, ghost_sum,
    table, pre, ghost_send, ghost_hot, dres, res_sum, wts, dsum,
    hot, picked, tsum, dt, table_sum, back_send, back_got, dpre,
    own_d, got_d, mid_d, last_d, own_u, got_u, mid_u, last_u, basis_got, basis_mid,
    half_send, half_got, far_send, far_got, res_mid, res_last, res_other,
    sem_ghost, sem_back, sem_d, sem_u, sem_basis, sem_core, sem_z, sem_far, sem_in, sem_out, edge_out, res_out, basis_out,
):
    slab, brick, near, far = where_am_i()
    core, z = lax.rem(near, 2), near // 2
    ahead = ((lax.rem(slab + 1, 8), brick), (lax.rem(slab + 7, 8), brick),
             (slab, lax.rem(brick + 1, 32)), (slab, lax.rem(brick + 31, 32)))
    behind = (ahead[1], ahead[0], ahead[3], ahead[2])
    loads = {}
    for place, (name, source, target) in enumerate((
        ("down", down_hbm, down_t), ("rows", rows_hbm, rows_out), ("w_res", w_res_hbm, w_res),
        ("cot", cot_hbm, cot), ("basis", basis_hbm, basis), ("w_basis", w_basis_hbm, w_basis), ("w_up", w_up_hbm, w_up),
        ("index", index_hbm, index), ("count", count_hbm, count),
    )):
        loads[name] = pltpu.make_async_copy(source, target, sem_in.at[place])
    quarters = [
        pltpu.make_async_copy(embed_hbm.at[256 * c : 256 * c + 256, :], embed.at[256 * c : 256 * c + 256, :], sem_in.at[9 + c])
        for c in range(4)
    ]
    loads["down"].start()
    for quarter in quarters:
        quarter.start()
    barrier = announce()
    loads["rows"].start()
    for name in ("w_res", "cot", "basis", "w_basis", "w_up", "index", "count"):
        loads[name].start()

    loads["down"].wait()
    for c in range(4):
        quarters[c].wait()
        part = dot(down_t[...], embed[256 * c : 256 * c + 256, :], 1, 1)
        pre[64 * c : 64 * c + 64, :] = part
        table[64 * c : 64 * c + 64, :] = (part * sigmoid(part)).astype(BF16)
    loads["rows"].wait()
    for k in range(4):
        sent = rows_out[k : k + 1, :]
        lanes = pl.ds(128 * k, 128)
        ghost_hot[:, lanes] = low_onehot(jnp.bitwise_and(sent, 255))
        wide = dot(table[0:256, :], ghost_hot[:, lanes])
        chunk = jnp.right_shift(sent, 8)
        chosen = wide[0:64]
        for c in range(1, 4):
            chosen = jnp.where(chunk == c, wide[64 * c : 64 * c + 64], chosen)
        ghost_send[k] = chosen.astype(BF16)
    pl.semaphore_wait(barrier, 32)

    def ghost_copy(k):
        place = table.at[pl.ds(256 + 64 * (k // 2), 64), pl.ds(128 * (k % 2), 128)]
        return remote(ghost_send.at[k], place, sem_ghost.at[0], sem_ghost.at[1], ahead[k])

    for k in range(4):
        ghost_copy(k).start()

    loads["w_res"].wait()
    loads["cot"].wait()

    def residual(i):
        rows = pl.ds(pl.multiple_of(256 * i, 256), 256)
        value = dot(embed[rows, :], w_res[...])
        dres[rows, :] = (cot[rows, :].astype(F32) * silu_grad(value)).astype(BF16)

    each(4, residual, 2)

    def residual_grad(i):
        rows = pl.ds(pl.multiple_of(128 * i, 128), 128)
        res_sum[rows, :] = dot(embed[:, rows], dres[...], 0, 0)

    each(4, residual_grad, 2)
    other_half = pl.ds(pl.multiple_of((1 - core) * 256, 256), 256)
    half_send[...] = res_sum[other_half, :].astype(BF16)
    core_first = remote(half_send, half_got, sem_core.at[0], sem_core.at[1], core_peer())
    core_first.start()

    for name in ("basis", "w_basis", "w_up", "index", "count"):
        loads[name].wait()
    w_t = w_basis[...].T
    dsum[...] = dot(w_up[...], cot[...], 1, 1)

    pltpu.make_async_copy(ghost_send, ghost_send, sem_ghost.at[1]).wait()
    tsum[...] = jnp.zeros_like(tsum)

    def gather(j):
        row = index[pl.ds(j, 1), :]
        low = jnp.where(j < count[...], jnp.bitwise_and(row, 255), -1)
        chunk = jnp.right_shift(row, 8)
        hot[j] = low_onehot(low)
        wide = dot(table[...], hot[j])
        chosen = wide[0:64]
        for c in range(1, 6):
            chosen = jnp.where(chunk == c, wide[64 * c : 64 * c + 64], chosen)
        picked[j] = chosen.astype(BF16)
        weights = dot(w_t, basis[pl.ds(pl.multiple_of(16 * j, 16), 16), :])
        wts[pl.ds(pl.multiple_of(64 * j, 64), 64), :] = weights
        tsum[...] += weights * chosen

    each(4, gather, 4)
    core_first.wait_recv()
    mine = pl.multiple_of(core * 256, 256)

    def to_far(t):
        rows = pl.ds(pl.multiple_of(mine + 16 * t, 16), 16)
        got = half_got[pl.ds(pl.multiple_of(16 * t, 16), 16), :]
        far_send[t] = (res_sum[rows, :] + got.astype(F32)).astype(BF16)

    each(16, to_far)
    res_scatter = Exchange(
        15, lambda s: far_send.at[lax.rem(far + s + 1, 16)], lambda s: far_got.at[s], far_got, far_got, (sem_far.at[0, 0], sem_far.at[1, 0]), far_peer
    )
    res_scatter.start()
    each(12, lambda j: gather(j + 4), 4)

    total = tsum[...]
    act = (total * sigmoid(total)).astype(BF16)
    dt[...] = dsum[...] * silu_grad(total)
    ghost_sum[...] = jnp.zeros_like(ghost_sum)
    table_sum[...] = jnp.zeros_like(table_sum)

    def only(chunk, c):
        return jnp.where(chunk == c, 1.0, 0.0).astype(BF16)

    def scatter_ghosts(j):
        chunk = jnp.right_shift(index[pl.ds(j, 1), :], 8)
        slope = dt[...]
        term = (slope * wts[pl.ds(pl.multiple_of(64 * j, 64), 64), :]).astype(BF16)
        terms[j] = term
        picked[j] = (slope * picked[j].astype(F32)).astype(BF16)
        parts = [term * only(chunk, c) for c in (4, 5)]
        ghost_sum[...] += dot(hot[j], jnp.concatenate(parts, axis=0), 1, 1)

    each(16, scatter_ghosts, 8)

    def back_copy(k):
        return remote(back_send.at[k], back_got.at[k], sem_back.at[0], sem_back.at[1], behind[k])

    ghost_rows = ghost_sum[...].T
    for k in range(4):
        back_send[k] = ghost_rows[64 * (k // 2) : 64 * (k // 2) + 64, 128 * (k % 2) : 128 * (k % 2) + 128].astype(BF16)
        back_copy(k).start()

    up_grad = dot(act, cot[...])
    for s in range(16):
        own_u[s] = up_grad[8 * (s // 2) : 8 * (s // 2) + 8, 256 * (s % 2) : 256 * (s % 2) + 256]
    sems_u = [(sem_u.at[0, t], sem_u.at[1, t]) for t in range(3)]
    scatter_u, middle_u, spread_u, final_u, gather_u = small_stages(own_u, got_u, mid_u, last_u, sems_u)
    scatter_u.start()

    res_scatter.arrived()
    mine_far = pl.ds(pl.multiple_of(16 * far, 16), 16)
    part = res_sum[pl.ds(pl.multiple_of(mine + 16 * far, 16), 16), :] + half_got[mine_far, :].astype(F32)
    for s in range(15):
        part = part + far_got[s].astype(F32)
    res_mid[z] = part.astype(BF16)
    res_spread = Exchange(7, lambda s: res_mid.at[z], lambda s: res_mid.at[z], res_mid.at[0:7], res_mid.at[0:7], (sem_z.at[0], sem_z.at[1]), z_peer)
    res_spread.start()
    def scatter_own(j):
        chunk = jnp.right_shift(index[pl.ds(j, 1), :], 8)
        parts = [terms[j] * only(chunk, c) for c in range(4)]
        table_sum[...] += dot(jnp.concatenate(parts, axis=0), hot[j], 1, 1)

    each(16, scatter_own, 8)
    basis_grad = jnp.zeros((16, 64), F32)
    for j in range(16):
        basis_grad = basis_grad + dot(basis[16 * j : 16 * j + 16, :], picked[j], 1, 1)
    basis_got[near] = jnp.concatenate([basis_grad[0:8], basis_grad[8:16]], axis=1)
    basis_a = Exchange(15, lambda s: basis_got.at[near], lambda s: basis_got.at[near], basis_got.at[0:15], basis_got.at[0:15], (sem_basis.at[0, 0], sem_basis.at[1, 0]), near_peer)
    basis_a.start()

    pltpu.make_async_copy(back_got, back_got, sem_back.at[1]).wait()
    columns = []
    for k in range(4):
        chunk = jnp.right_shift(rows_out[k : k + 1, :], 8)
        term = back_got[k]
        columns.append(jnp.concatenate([term * only(chunk, c) for c in range(4)], axis=0))
    returned = table_sum[...] + dot(jnp.concatenate(columns, axis=1), ghost_hot[...], 1, 1)
    returned = (returned * silu_grad(pre[...])).astype(BF16)
    for c in range(4):
        dpre[:, 256 * c : 256 * c + 256] = returned[64 * c : 64 * c + 64, :]
    down_grad = dot(dpre[...], embed[...])
    for s in range(16):
        own_d[s] = down_grad[8 * (s // 2) : 8 * (s // 2) + 8, 256 * (s % 2) : 256 * (s % 2) + 256]
    sems_d = [(sem_d.at[0, t], sem_d.at[1, t]) for t in range(3)]
    scatter_d, middle_d, spread_d, final_d, gather_d = small_stages(own_d, got_d, mid_d, last_d, sems_d)
    scatter_d.start()

    def edge(i):
        rows = pl.ds(pl.multiple_of(256 * i, 256), 256)
        value = dot(dres[rows, :], w_res[...], 1, 1) + dot(dpre[:, rows], down_t[...], 0, 0)
        edge_out[rows, :] = value.astype(BF16)

    each(4, edge, 2)
    edge_copy = pltpu.make_async_copy(edge_out, edge_hbm, sem_out.at[0])
    edge_copy.start()

    middle_u()
    spread_u.start()
    middle_d()
    spread_d.start()
    res_spread.arrived()
    part = res_mid[0].astype(F32)
    for s in range(1, 8):
        part = part + res_mid[s].astype(F32)
    res_last[mine_far, :] = part.astype(BF16)
    res_gather = Exchange(
        15, lambda s: res_last.at[mine_far, :], lambda s: res_last.at[mine_far, :], res_last.at[0:240], res_last.at[0:240], (sem_far.at[0, 1], sem_far.at[1, 1]), far_peer
    )
    res_gather.start()

    final_u()
    gather_u.start()
    basis_a.arrived()
    basis_total = basis_got[0]
    for s in range(1, 16):
        basis_total = basis_total + basis_got[s]
    basis_mid[far] = basis_total
    basis_b = Exchange(15, lambda s: basis_mid.at[far], lambda s: basis_mid.at[far], basis_mid.at[0:15], basis_mid.at[0:15], (sem_basis.at[0, 1], sem_basis.at[1, 1]), far_peer)
    basis_b.start()

    final_d()
    gather_d.start()
    res_gather.arrived()
    core_last = remote(res_last, res_other, sem_core.at[2], sem_core.at[3], core_peer())
    core_last.start()
    res_out[pl.ds(mine, 256), :] = res_last[...].astype(F32)
    basis_b.arrived()
    basis_total = basis_mid[0]
    for s in range(1, 16):
        basis_total = basis_total + basis_mid[s]
    basis_out[...] = jnp.concatenate([basis_total[:, 0:64], basis_total[:, 64:128]], axis=0)
    basis_copy = pltpu.make_async_copy(basis_out, basis_dest, sem_out.at[2])
    basis_copy.start()
    gather_u.arrived()
    for s in range(16):
        small_out[64 + 8 * (s // 2) : 72 + 8 * (s // 2), 256 * (s % 2) : 256 * (s % 2) + 256] = last_u[s].astype(F32)
    core_last.wait_recv()
    res_out[other_half, :] = res_other[...].astype(F32)
    res_copy = pltpu.make_async_copy(res_out, res_hbm, sem_out.at[1])
    res_copy.start()
    pltpu.make_async_copy(ghost_send, ghost_send, sem_ghost.at[0]).wait()
    pltpu.make_async_copy(back_send, back_send, sem_back.at[0]).wait()
    for exchange in (scatter_u, spread_u, gather_u, scatter_d, spread_d, basis_a, basis_b, res_scatter, res_spread, res_gather):
        exchange.sent()
    core_first.wait_send()
    core_last.wait_send()
    gather_d.arrived()
    for s in range(16):
        small_out[8 * (s // 2) : 8 * (s // 2) + 8, 256 * (s % 2) : 256 * (s % 2) + 256] = last_d[s].astype(F32)
    gather_d.sent()
    edge_copy.wait()
    res_copy.wait()
    basis_copy.wait()


def copy_kernel(edge, res, small, basis, edge_out, res_out, down_out, up_out, basis_out, sems):
    pairs = [(small.at[0:64, :], down_out), (small.at[64:128, :], up_out), (basis, basis_out)]
    for k in range(4):
        pairs.append((edge.at[256 * k : 256 * k + 256, :], edge_out.at[256 * k : 256 * k + 256, :]))
        pairs.append((res.at[128 * k : 128 * k + 128, :], res_out.at[128 * k : 128 * k + 128, :]))
    copies = [pltpu.make_async_copy(source, target, sems.at[k]) for k, (source, target) in enumerate(pairs)]
    for copy in copies:
        copy.start()
    for copy in copies:
        copy.wait()


def hand_over(edge, res, small, basis):
    shapes = (((1024, 512), BF16), ((512, 512), F32), ((64, 512), F32), ((64, 512), F32), ((16, 64), F32))
    return pl.pallas_call(
        copy_kernel,
        out_shape=tuple(jax.ShapeDtypeStruct(*shape) for shape in shapes),
        in_specs=[pl.BlockSpec(memory_space=pl.ANY)] * 4,
        out_specs=[pl.BlockSpec(memory_space=pl.ANY)] * 5,
        scratch_shapes=[DMA((11,))],
        compiler_params=pltpu.CompilerParams(vmem_limit_bytes=8 * 1024 * 1024),
        name="hand_over",
    )(edge, res, small, basis)


def shards(
    embed, cotangent, basis, triplet_row_index, triplet_slot_count, outgoing_edge_rows,
    residual_weight, down_weight, up_weight, basis_weight,
):
    vmem = pltpu.VMEM
    edge, res, small, base = pl.pallas_call(
        fused_kernel,
        out_shape=(
            vmem((1024, 512), BF16),
            vmem((512, 512), F32),
            vmem((128, 512), F32),
            vmem((16, 64), F32),
        ),
        in_specs=[pl.BlockSpec(memory_space=pltpu.HBM)] * 10,
        out_specs=[pl.BlockSpec(memory_space=pl.ANY), pl.BlockSpec(memory_space=pl.ANY), pl.BlockSpec(memory_space=vmem), pl.BlockSpec(memory_space=pl.ANY)],
        scratch_shapes=[
            vmem((1024, 512), BF16),
            vmem((1024, 512), BF16),
            vmem((256, 1024), BF16),
            vmem((16, 1024), jnp.int32),
            vmem((1, 1024), jnp.int32),
            vmem((4, 128), jnp.int32),
            vmem((512, 512), BF16),
            vmem((64, 512), BF16),
            vmem((64, 512), BF16),
            vmem((16, 64), BF16),
            vmem((16, 64, 1024), BF16),
            vmem((256, 128), F32),
            vmem((384, 256), BF16),
            vmem((256, 256), F32),
            vmem((4, 64, 128), BF16),
            vmem((256, 512), BF16),
            vmem((1024, 512), BF16),
            vmem((512, 512), F32),
            vmem((1024, 1024), F32),
            vmem((64, 1024), F32),
            vmem((16, 256, 1024), BF16),
            vmem((16, 64, 1024), BF16),
            vmem((64, 1024), F32),
            vmem((64, 1024), F32),
            vmem((256, 256), F32),
            vmem((4, 64, 128), BF16),
            vmem((4, 64, 128), BF16),
            vmem((64, 1024), BF16),
            vmem((16, 8, 256), F32),
            vmem((15, 8, 256), F32),
            vmem((16, 8, 256), BF16),
            vmem((16, 8, 256), BF16),
            vmem((16, 8, 256), F32),
            vmem((15, 8, 256), F32),
            vmem((16, 8, 256), BF16),
            vmem((16, 8, 256), BF16),
            vmem((16, 8, 128), F32),
            vmem((16, 8, 128), F32),
            vmem((256, 512), BF16),
            vmem((256, 512), BF16),
            vmem((16, 16, 512), BF16),
            vmem((15, 16, 512), BF16),
            vmem((8, 16, 512), BF16),
            vmem((256, 512), BF16),
            vmem((256, 512), BF16),
            DMA((2,)),
            DMA((2,)),
            DMA((2, 3)),
            DMA((2, 3)),
            DMA((2, 2)),
            DMA((4,)),
            DMA((2,)),
            DMA((2, 2)),
            DMA((13,)),
            DMA((3,)),
            vmem((1024, 512), BF16),
            vmem((512, 512), F32),
            vmem((16, 64), F32),
        ],
        compiler_params=pltpu.CompilerParams(
            collective_id=0, has_side_effects=True, vmem_limit_bytes=40 * 1024 * 1024
        ),
        name="fused",
    )(
        *(
            pltpu.with_memory_space_constraint(value, pltpu.HBM)
            for value in (
                embed, cotangent, basis.reshape(256, 1024), triplet_row_index, triplet_slot_count.reshape(1, 1024),
                outgoing_edge_rows, residual_weight, down_weight.T, up_weight, basis_weight,
            )
        )
    )
    edge, res, down, up, base = hand_over(edge, res, small, base)
    return edge, res, down.T, up, base


def solution(mesh):
    in_specs = (
        P(("slab", "brick"), None),
        P(("slab", "brick"), None),
        P(None, None, ("slab", "brick")),
        P(None, ("slab", "brick")),
        P(("slab", "brick")),
        P(None, ("slab", "brick")),
        P(),
        P(),
        P(),
        P(),
    )
    out_specs = (P(("slab", "brick"), None), P(), P(), P(), P())
    return jax.shard_map(shards, mesh=mesh, in_specs=in_specs, out_specs=out_specs, check_vma=False)
```

```python
import functools

import jax
import jax.numpy as jnp
from jax import lax
from jax.experimental import pallas as pl
from jax.experimental.pallas import tpu as pltpu
from jax.sharding import PartitionSpec as P

MESH = pl.DeviceIdType.MESH
DMA = pltpu.SemaphoreType.DMA


def where_am_i():
    slab, brick = lax.axis_index("slab"), lax.axis_index("brick")
    near = lax.rem(brick, 16)
    far = slab * 2 + brick // 16
    return slab, brick, near, far


def near_peer(step):
    slab, brick, near, _ = where_am_i()
    return slab, (brick // 16) * 16 + lax.rem(near + step, 16)


def far_peer(step):
    _, _, near, far = where_am_i()
    other = lax.rem(far + step, 16)
    return other // 2, lax.rem(other, 2) * 16 + near


def z_peer(step):
    slab, brick, near, _ = where_am_i()
    return slab, (brick // 16) * 16 + lax.rem(near + 2 * step, 16)


def core_peer():
    slab, brick, _, _ = where_am_i()
    return slab, brick + 1 - 2 * lax.rem(brick, 2)


def remote(source, target, send, recv, peer):
    return pltpu.make_async_remote_copy(
        src_ref=source, dst_ref=target, send_sem=send, recv_sem=recv,
        device_id=peer, device_id_type=MESH,
    )


def each(count, body, unroll=1):
    def step(index, carry):
        body(index)
        return carry

    lax.fori_loop(0, count, step, 0, unroll=unroll)


FARTHEST_FIRST = {
    near_peer: (8, 7, 9, 6, 10, 5, 11, 4, 12, 3, 13, 2, 14, 1, 15),
    far_peer: (3, 13, 5, 11, 4, 12, 1, 15, 6, 10, 7, 9, 2, 14, 8),
    z_peer: (4, 3, 5, 2, 6, 1, 7),
}


class Exchange:
    def __init__(self, count, source, target, gone, came, sems, peer):
        self.count, self.source, self.target, self.gone, self.came = count, source, target, gone, came
        self.sems, self.peer = sems, peer

    def start(self):
        send, recv = self.sems
        for step in FARTHEST_FIRST[self.peer]:
            s = step - 1
            remote(self.source(s), self.target(s), send, recv, self.peer(step)).start()

    def arrived(self):
        pltpu.make_async_copy(self.came, self.came, self.sems[1]).wait()

    def sent(self):
        pltpu.make_async_copy(self.gone, self.gone, self.sems[0]).wait()


def small_stages(own, got, mid, last, sems):
    _, _, near, far = where_am_i()
    scatter = Exchange(
        15, lambda s: own.at[lax.rem(far + s + 1, 16)], lambda s: got.at[s], got, got, sems[0], far_peer
    )
    spread = Exchange(15, lambda s: mid.at[near], lambda s: mid.at[near], mid.at[0:15], mid.at[0:15], sems[1], near_peer)
    gather = Exchange(15, lambda s: last.at[far], lambda s: last.at[far], last.at[0:15], last.at[0:15], sems[2], far_peer)

    def middle():
        scatter.arrived()
        total = own[far]
        for s in range(15):
            total = total + got[s]
        mid[near] = total.astype(mid.dtype)

    def final():
        spread.arrived()
        total = mid[0].astype(F32)
        for s in range(1, 16):
            total = total + mid[s].astype(F32)
        last[far] = total.astype(last.dtype)

    return scatter, middle, spread, final, gather


def announce():
    slab, brick, _, _ = where_am_i()
    barrier = pltpu.get_barrier_semaphore()

    def tell(peer):
        pl.semaphore_signal(barrier, inc=1, device_id=peer, device_id_type=MESH)

    for peer in (near_peer, far_peer):
        for step in FARTHEST_FIRST[peer]:
            tell(peer(step))
    tell((slab, lax.rem(brick + 1, 32)))
    tell((slab, lax.rem(brick + 31, 32)))
    return barrier


F32, BF16 = jnp.float32, jnp.bfloat16


def sigmoid(value):
    return 0.5 * jnp.tanh(0.5 * value) + 0.5


def silu_grad(value):
    sig = sigmoid(value)
    return sig * (1.0 + value * (1.0 - sig))


def dot(a, b, ca=1, cb=0):
    return lax.dot_general(a, b, (((ca,), (cb,)), ((), ())), preferred_element_type=F32)


def low_onehot(low):
    width = low.shape[1]
    positions = lax.broadcasted_iota(jnp.int32, (256, width), 0).astype(F32).astype(BF16)
    return jnp.where(positions == low.astype(F32).astype(BF16), jnp.ones((), BF16), jnp.zeros((), BF16))


def slice_of(s):
    return pl.ds(8 * (s // 2), 8), pl.ds(256 * (s % 2), 256)


def fused_kernel(
    embed_hbm, cot_hbm, basis_hbm, index_hbm, count_hbm, rows_hbm, w_res_hbm, down_hbm, w_up_hbm, w_basis_hbm,
    edge_hbm, res_hbm, small_out, basis_dest,
    embed, cot, basis, index, count, rows_out, w_res, down_t, w_up, w_basis,
    terms, ghost_sum,
    table, pre, ghost_send, ghost_hot, dres, res_sum, wts, dsum,
    hot, picked, tsum, dt, table_sum, back_send, back_got, dpre,
    own_d, got_d, mid_d, last_d, own_u, got_u, mid_u, last_u, basis_got, basis_mid,
    half_send, half_got, far_send, far_got, res_mid, res_last, res_other,
    sem_ghost, sem_back, sem_d, sem_u, sem_basis, sem_core, sem_z, sem_far, sem_in, sem_out, edge_out, res_out, basis_out,
):
    slab, brick, near, far = where_am_i()
    core, z = lax.rem(near, 2), near // 2
    ahead = ((lax.rem(slab + 1, 8), brick), (lax.rem(slab + 7, 8), brick),
             (slab, lax.rem(brick + 1, 32)), (slab, lax.rem(brick + 31, 32)))
    behind = (ahead[1], ahead[0], ahead[3], ahead[2])
    loads = {}
    for place, (name, source, target) in enumerate((
        ("down", down_hbm, down_t), ("rows", rows_hbm, rows_out), ("w_res", w_res_hbm, w_res),
        ("cot", cot_hbm, cot), ("basis", basis_hbm, basis), ("w_basis", w_basis_hbm, w_basis), ("w_up", w_up_hbm, w_up),
        ("index", index_hbm, index), ("count", count_hbm, count),
    )):
        loads[name] = pltpu.make_async_copy(source, target, sem_in.at[place])
    quarters = [
        pltpu.make_async_copy(embed_hbm.at[256 * c : 256 * c + 256, :], embed.at[256 * c : 256 * c + 256, :], sem_in.at[9 + c])
        for c in range(4)
    ]
    loads["down"].start()
    for quarter in quarters:
        quarter.start()
    barrier = announce()
    loads["rows"].start()
    for name in ("w_res", "cot", "basis", "w_basis", "w_up", "index", "count"):
        loads[name].start()

    loads["down"].wait()
    for c in range(4):
        quarters[c].wait()
        part = dot(down_t[...], embed[256 * c : 256 * c + 256, :], 1, 1)
        pre[64 * c : 64 * c + 64, :] = part
        table[64 * c : 64 * c + 64, :] = (part * sigmoid(part)).astype(BF16)
    loads["rows"].wait()
    for k in range(4):
        sent = rows_out[k : k + 1, :]
        lanes = pl.ds(128 * k, 128)
        ghost_hot[:, lanes] = low_onehot(jnp.bitwise_and(sent, 255))
        wide = dot(table[0:256, :], ghost_hot[:, lanes])
        chunk = jnp.right_shift(sent, 8)
        chosen = wide[0:64]
        for c in range(1, 4):
            chosen = jnp.where(chunk == c, wide[64 * c : 64 * c + 64], chosen)
        ghost_send[k] = chosen.astype(BF16)
    pl.semaphore_wait(barrier, 32)

    def ghost_copy(k):
        place = table.at[pl.ds(256 + 64 * (k // 2), 64), pl.ds(128 * (k % 2), 128)]
        return remote(ghost_send.at[k], place, sem_ghost.at[0], sem_ghost.at[1], ahead[k])

    for k in (2, 3, 0, 1):
        ghost_copy(k).start()

    loads["w_res"].wait()
    loads["cot"].wait()

    def residual(i):
        rows = pl.ds(pl.multiple_of(256 * i, 256), 256)
        value = dot(embed[rows, :], w_res[...])
        dres[rows, :] = (cot[rows, :].astype(F32) * silu_grad(value)).astype(BF16)

    each(4, residual, 2)

    def residual_grad(i):
        rows = pl.ds(pl.multiple_of(128 * i, 128), 128)
        res_sum[rows, :] = dot(embed[:, rows], dres[...], 0, 0)

    each(4, residual_grad, 2)
    other_half = pl.ds(pl.multiple_of((1 - core) * 256, 256), 256)
    half_send[...] = res_sum[other_half, :].astype(BF16)
    core_first = remote(half_send, half_got, sem_core.at[0], sem_core.at[1], core_peer())
    core_first.start()

    for name in ("basis", "w_basis", "w_up", "index", "count"):
        loads[name].wait()
    w_t = w_basis[...].T
    dsum[...] = dot(w_up[...], cot[...], 1, 1)

    pltpu.make_async_copy(ghost_send, ghost_send, sem_ghost.at[1]).wait()
    tsum[...] = jnp.zeros_like(tsum)

    def gather(j):
        row = index[pl.ds(j, 1), :]
        low = jnp.where(j < count[...], jnp.bitwise_and(row, 255), -1)
        chunk = jnp.right_shift(row, 8)
        hot[j] = low_onehot(low)
        wide = dot(table[...], hot[j])
        chosen = wide[0:64]
        for c in range(1, 6):
            chosen = jnp.where(chunk == c, wide[64 * c : 64 * c + 64], chosen)
        picked[j] = chosen.astype(BF16)
        weights = dot(w_t, basis[pl.ds(pl.multiple_of(16 * j, 16), 16), :])
        wts[pl.ds(pl.multiple_of(64 * j, 64), 64), :] = weights
        tsum[...] += weights * chosen

    each(4, gather, 4)
    core_first.wait_recv()
    mine = pl.multiple_of(core * 256, 256)

    def to_far(t):
        rows = pl.ds(pl.multiple_of(mine + 16 * t, 16), 16)
        got = half_got[pl.ds(pl.multiple_of(16 * t, 16), 16), :]
        far_send[t] = (res_sum[rows, :] + got.astype(F32)).astype(BF16)

    each(16, to_far)
    res_scatter = Exchange(
        15, lambda s: far_send.at[lax.rem(far + s + 1, 16)], lambda s: far_got.at[s], far_got, far_got, (sem_far.at[0, 0], sem_far.at[1, 0]), far_peer
    )
    res_scatter.start()
    each(12, lambda j: gather(j + 4), 4)

    total = tsum[...]
    act = (total * sigmoid(total)).astype(BF16)
    dt[...] = dsum[...] * silu_grad(total)
    ghost_sum[...] = jnp.zeros_like(ghost_sum)
    table_sum[...] = jnp.zeros_like(table_sum)

    def only(chunk, c):
        return jnp.where(chunk == c, 1.0, 0.0).astype(BF16)

    def scatter_ghosts(j):
        chunk = jnp.right_shift(index[pl.ds(j, 1), :], 8)
        slope = dt[...]
        term = (slope * wts[pl.ds(pl.multiple_of(64 * j, 64), 64), :]).astype(BF16)
        terms[j] = term
        picked[j] = (slope * picked[j].astype(F32)).astype(BF16)
        parts = [term * only(chunk, c) for c in (4, 5)]
        ghost_sum[...] += dot(hot[j], jnp.concatenate(parts, axis=0), 1, 1)

    each(16, scatter_ghosts, 8)

    def back_copy(k):
        return remote(back_send.at[k], back_got.at[k], sem_back.at[0], sem_back.at[1], behind[k])

    ghost_rows = ghost_sum[...].T
    for k in (2, 3, 0, 1):
        back_send[k] = ghost_rows[64 * (k // 2) : 64 * (k // 2) + 64, 128 * (k % 2) : 128 * (k % 2) + 128].astype(BF16)
        back_copy(k).start()

    up_grad = dot(act, cot[...])
    for s in range(16):
        own_u[s] = up_grad[8 * (s // 2) : 8 * (s // 2) + 8, 256 * (s % 2) : 256 * (s % 2) + 256]
    sems_u = [(sem_u.at[0, t], sem_u.at[1, t]) for t in range(3)]
    scatter_u, middle_u, spread_u, final_u, gather_u = small_stages(own_u, got_u, mid_u, last_u, sems_u)
    scatter_u.start()

    res_scatter.arrived()
    mine_far = pl.ds(pl.multiple_of(16 * far, 16), 16)
    part = res_sum[pl.ds(pl.multiple_of(mine + 16 * far, 16), 16), :] + half_got[mine_far, :].astype(F32)
    for s in range(15):
        part = part + far_got[s].astype(F32)
    res_mid[z] = part.astype(BF16)
    res_spread = Exchange(7, lambda s: res_mid.at[z], lambda s: res_mid.at[z], res_mid.at[0:7], res_mid.at[0:7], (sem_z.at[0], sem_z.at[1]), z_peer)
    res_spread.start()
    def scatter_own(j):
        chunk = jnp.right_shift(index[pl.ds(j, 1), :], 8)
        parts = [terms[j] * only(chunk, c) for c in range(4)]
        table_sum[...] += dot(jnp.concatenate(parts, axis=0), hot[j], 1, 1)

    each(16, scatter_own, 8)
    basis_grad = jnp.zeros((16, 64), F32)
    for j in range(16):
        basis_grad = basis_grad + dot(basis[16 * j : 16 * j + 16, :], picked[j], 1, 1)
    basis_got[near] = jnp.concatenate([basis_grad[0:8], basis_grad[8:16]], axis=1)
    basis_a = Exchange(15, lambda s: basis_got.at[near], lambda s: basis_got.at[near], basis_got.at[0:15], basis_got.at[0:15], (sem_basis.at[0, 0], sem_basis.at[1, 0]), near_peer)
    basis_a.start()

    pltpu.make_async_copy(back_got, back_got, sem_back.at[1]).wait()
    columns = []
    for k in range(4):
        chunk = jnp.right_shift(rows_out[k : k + 1, :], 8)
        term = back_got[k]
        columns.append(jnp.concatenate([term * only(chunk, c) for c in range(4)], axis=0))
    returned = table_sum[...] + dot(jnp.concatenate(columns, axis=1), ghost_hot[...], 1, 1)
    returned = (returned * silu_grad(pre[...])).astype(BF16)
    for c in range(4):
        dpre[:, 256 * c : 256 * c + 256] = returned[64 * c : 64 * c + 64, :]
    down_grad = dot(dpre[...], embed[...])
    for s in range(16):
        own_d[s] = down_grad[8 * (s // 2) : 8 * (s // 2) + 8, 256 * (s % 2) : 256 * (s % 2) + 256]
    sems_d = [(sem_d.at[0, t], sem_d.at[1, t]) for t in range(3)]
    scatter_d, middle_d, spread_d, final_d, gather_d = small_stages(own_d, got_d, mid_d, last_d, sems_d)
    scatter_d.start()

    def edge(i):
        rows = pl.ds(pl.multiple_of(256 * i, 256), 256)
        value = dot(dres[rows, :], w_res[...], 1, 1) + dot(dpre[:, rows], down_t[...], 0, 0)
        edge_out[rows, :] = value.astype(BF16)

    each(4, edge, 2)
    edge_copy = pltpu.make_async_copy(edge_out, edge_hbm, sem_out.at[0])
    edge_copy.start()

    middle_u()
    spread_u.start()
    middle_d()
    spread_d.start()
    res_spread.arrived()
    part = res_mid[0].astype(F32)
    for s in range(1, 8):
        part = part + res_mid[s].astype(F32)
    res_last[mine_far, :] = part.astype(BF16)
    res_gather = Exchange(
        15, lambda s: res_last.at[mine_far, :], lambda s: res_last.at[mine_far, :], res_last.at[0:240], res_last.at[0:240], (sem_far.at[0, 1], sem_far.at[1, 1]), far_peer
    )
    res_gather.start()

    final_u()
    gather_u.start()
    basis_a.arrived()
    basis_total = basis_got[0]
    for s in range(1, 16):
        basis_total = basis_total + basis_got[s]
    basis_mid[far] = basis_total
    basis_b = Exchange(15, lambda s: basis_mid.at[far], lambda s: basis_mid.at[far], basis_mid.at[0:15], basis_mid.at[0:15], (sem_basis.at[0, 1], sem_basis.at[1, 1]), far_peer)
    basis_b.start()

    final_d()
    gather_d.start()
    res_gather.arrived()
    core_last = remote(res_last, res_other, sem_core.at[2], sem_core.at[3], core_peer())
    core_last.start()
    res_out[pl.ds(mine, 256), :] = res_last[...].astype(F32)
    basis_b.arrived()
    basis_total = basis_mid[0]
    for s in range(1, 16):
        basis_total = basis_total + basis_mid[s]
    basis_out[...] = jnp.concatenate([basis_total[:, 0:64], basis_total[:, 64:128]], axis=0)
    basis_copy = pltpu.make_async_copy(basis_out, basis_dest, sem_out.at[2])
    basis_copy.start()
    gather_u.arrived()
    for s in range(16):
        small_out[64 + 8 * (s // 2) : 72 + 8 * (s // 2), 256 * (s % 2) : 256 * (s % 2) + 256] = last_u[s].astype(F32)
    core_last.wait_recv()
    res_out[other_half, :] = res_other[...].astype(F32)
    res_copy = pltpu.make_async_copy(res_out, res_hbm, sem_out.at[1])
    res_copy.start()
    pltpu.make_async_copy(ghost_send, ghost_send, sem_ghost.at[0]).wait()
    pltpu.make_async_copy(back_send, back_send, sem_back.at[0]).wait()
    for exchange in (scatter_u, spread_u, gather_u, scatter_d, spread_d, basis_a, basis_b, res_scatter, res_spread, res_gather):
        exchange.sent()
    core_first.wait_send()
    core_last.wait_send()
    gather_d.arrived()
    for s in range(16):
        small_out[8 * (s // 2) : 8 * (s // 2) + 8, 256 * (s % 2) : 256 * (s % 2) + 256] = last_d[s].astype(F32)
    gather_d.sent()
    edge_copy.wait()
    res_copy.wait()
    basis_copy.wait()


def copy_kernel(edge, res, small, basis, edge_out, res_out, down_out, up_out, basis_out, sems):
    pairs = [(small.at[0:64, :], down_out), (small.at[64:128, :], up_out), (basis, basis_out)]
    for k in range(4):
        pairs.append((edge.at[256 * k : 256 * k + 256, :], edge_out.at[256 * k : 256 * k + 256, :]))
        pairs.append((res.at[128 * k : 128 * k + 128, :], res_out.at[128 * k : 128 * k + 128, :]))
    copies = [pltpu.make_async_copy(source, target, sems.at[k]) for k, (source, target) in enumerate(pairs)]
    for copy in copies:
        copy.start()
    for copy in copies:
        copy.wait()


def hand_over(edge, res, small, basis):
    shapes = (((1024, 512), BF16), ((512, 512), F32), ((64, 512), F32), ((64, 512), F32), ((16, 64), F32))
    return pl.pallas_call(
        copy_kernel,
        out_shape=tuple(jax.ShapeDtypeStruct(*shape) for shape in shapes),
        in_specs=[pl.BlockSpec(memory_space=pl.ANY)] * 4,
        out_specs=[pl.BlockSpec(memory_space=pl.ANY)] * 5,
        scratch_shapes=[DMA((11,))],
        compiler_params=pltpu.CompilerParams(vmem_limit_bytes=8 * 1024 * 1024),
        name="hand_over",
    )(edge, res, small, basis)


def shards(
    embed, cotangent, basis, triplet_row_index, triplet_slot_count, outgoing_edge_rows,
    residual_weight, down_weight, up_weight, basis_weight,
):
    vmem = pltpu.VMEM
    edge, res, small, base = pl.pallas_call(
        fused_kernel,
        out_shape=(
            vmem((1024, 512), BF16),
            vmem((512, 512), F32),
            vmem((128, 512), F32),
            vmem((16, 64), F32),
        ),
        in_specs=[pl.BlockSpec(memory_space=pltpu.HBM)] * 10,
        out_specs=[pl.BlockSpec(memory_space=pl.ANY), pl.BlockSpec(memory_space=pl.ANY), pl.BlockSpec(memory_space=vmem), pl.BlockSpec(memory_space=pl.ANY)],
        scratch_shapes=[
            vmem((1024, 512), BF16),
            vmem((1024, 512), BF16),
            vmem((256, 1024), BF16),
            vmem((16, 1024), jnp.int32),
            vmem((1, 1024), jnp.int32),
            vmem((4, 128), jnp.int32),
            vmem((512, 512), BF16),
            vmem((64, 512), BF16),
            vmem((64, 512), BF16),
            vmem((16, 64), BF16),
            vmem((16, 64, 1024), BF16),
            vmem((256, 128), F32),
            vmem((384, 256), BF16),
            vmem((256, 256), F32),
            vmem((4, 64, 128), BF16),
            vmem((256, 512), BF16),
            vmem((1024, 512), BF16),
            vmem((512, 512), F32),
            vmem((1024, 1024), F32),
            vmem((64, 1024), F32),
            vmem((16, 256, 1024), BF16),
            vmem((16, 64, 1024), BF16),
            vmem((64, 1024), F32),
            vmem((64, 1024), F32),
            vmem((256, 256), F32),
            vmem((4, 64, 128), BF16),
            vmem((4, 64, 128), BF16),
            vmem((64, 1024), BF16),
            vmem((16, 8, 256), F32),
            vmem((15, 8, 256), F32),
            vmem((16, 8, 256), BF16),
            vmem((16, 8, 256), BF16),
            vmem((16, 8, 256), F32),
            vmem((15, 8, 256), F32),
            vmem((16, 8, 256), BF16),
            vmem((16, 8, 256), BF16),
            vmem((16, 8, 128), F32),
            vmem((16, 8, 128), F32),
            vmem((256, 512), BF16),
            vmem((256, 512), BF16),
            vmem((16, 16, 512), BF16),
            vmem((15, 16, 512), BF16),
            vmem((8, 16, 512), BF16),
            vmem((256, 512), BF16),
            vmem((256, 512), BF16),
            DMA((2,)),
            DMA((2,)),
            DMA((2, 3)),
            DMA((2, 3)),
            DMA((2, 2)),
            DMA((4,)),
            DMA((2,)),
            DMA((2, 2)),
            DMA((13,)),
            DMA((3,)),
            vmem((1024, 512), BF16),
            vmem((512, 512), F32),
            vmem((16, 64), F32),
        ],
        compiler_params=pltpu.CompilerParams(
            collective_id=0, has_side_effects=True, vmem_limit_bytes=40 * 1024 * 1024
        ),
        name="fused",
    )(
        *(
            pltpu.with_memory_space_constraint(value, pltpu.HBM)
            for value in (
                embed, cotangent, basis.reshape(256, 1024), triplet_row_index, triplet_slot_count.reshape(1, 1024),
                outgoing_edge_rows, residual_weight, down_weight.T, up_weight, basis_weight,
            )
        )
    )
    edge, res, down, up, base = hand_over(edge, res, small, base)
    return edge, res, down.T, up, base


def solution(mesh):
    in_specs = (
        P(("slab", "brick"), None),
        P(("slab", "brick"), None),
        P(None, None, ("slab", "brick")),
        P(None, ("slab", "brick")),
        P(("slab", "brick")),
        P(None, ("slab", "brick")),
        P(),
        P(),
        P(),
        P(),
    )
    out_specs = (P(("slab", "brick"), None), P(), P(), P(), P())
    return jax.shard_map(shards, mesh=mesh, in_specs=in_specs, out_specs=out_specs, check_vma=False)
```
